32 devices in a mesh: group: 4 (over y, x), shard: 8 (over z, core).
Axes of the slice: x: 2, y: 2, z: 4, core: 2. Of those that a mesh axis runs over, the one named last changes fastest.
Arguments:
- tokens: bfloat16 [32, 192, 768], P(('group', 'shard')), may hold values from -650 to 650
- norm_gain: float32 [768], replicated, may hold values from 0.1 to 1.9
- w_query: bfloat16 [768, 768], P('shard'), may hold values from -8 to 8
- w_key: bfloat16 [768, 768], P('shard'), may hold values from -0.21875 to 0.21875
- w_value: bfloat16 [768, 768], P('shard'), may hold values from -0.625 to 0.625
- w_out: bfloat16 [768, 768], P('shard'), may hold values from -0.21875 to 0.21875
- owner_map: int32 [4, 8], P('group'), may hold values from 0 to 7, each once within a row
- pair_images: int32 [256, 2], P(('group', 'shard')), may hold values from 0 to 7, as said below
- pair_count: int32 [32], P(('group', 'shard')), may hold values from 1 to 8, 128 in all
- confidence: int32 [256, 2], P(('group', 'shard')), may hold values from 1 to 8
Outputs:
- updated: bfloat16 [32, 192, 768], P(('group', 'shard'))
The draws below stay inside these ranges and needn't reach their ends.
Inputs may be any that keep to these rules, and one draw needn't show every extreme that they name: `pair_images`: each row names two different images of the listing device's own group, by their index within that group. Device d lists its pairs in its first pair_count[d] rows of pair_images and confidence; the other rows are unused.
All inputs are finite; a program needn't handle non-finite values.
Results may differ from the reference program's by a relative error of at most 0.013.
The reference program's roundings to bfloat16 on the way (of `normed`, `query`, `attention` and `attended`) count: a program that leaves them out, or rounds other values in their place, can miss the bound.
Values may be sent and summed in bfloat16 or wider, within the bound.
No kernel may reach another device: no remote copies, remote signals or barrier semaphores. Data moves between devices by JAX's collectives and lax.ppermute only.
A program may use at most 128 MiB of HBM per device.

```python
import math
import jax
import jax.numpy as jnp
import numpy as np
from jax import lax

D = 768
HEADS = 12
HEAD_DIM = 64
SEQ = 192
PAIR_CAP = 8
IMAGES = 32
SLOTS = 256
PAIRS = 128
N_GROUP = 4
N_SHARD = 8
DEVICES = 32


def draw_tokens(key, part):
    first = jax.random.fold_in(jax.random.fold_in(key, 11), 0)
    values = jnp.clip(jax.random.normal(first, (IMAGES, SEQ, D), jnp.float32), -6.0, 6.0)
    return values.astype(jnp.bfloat16)


def draw_w_query(key, part):
    values = jax.random.normal(jax.random.fold_in(key, 23), (D, D), jnp.float32) * D ** (-0.5)
    return jnp.clip(values, -8.0, 8.0).astype(jnp.bfloat16)


def draw_pair_images(key, part):
    first, second = jax.random.split(jax.random.fold_in(key, 37))
    left = jax.random.randint(first, (SLOTS, 1), 0, N_SHARD, dtype=jnp.int32)
    offset = jax.random.randint(second, (SLOTS, 1), 1, N_SHARD, dtype=jnp.int32)
    return jnp.concatenate([left, (left + offset) % N_SHARD], axis=1)


def plant(values, stream_key, smallest, high):
    longest = values.shape.index(max(values.shape))
    spots = []
    for shift in (0, 1):
        where = [jax.random.randint(jax.random.fold_in(stream_key, axis), (), 0, length) for axis, length in enumerate(values.shape)]
        where[longest] = (where[longest] + shift) % values.shape[longest]
        spots.append(tuple(where))
    return values.at[spots[0]].set(smallest).at[spots[1]].set(high)


def level_of(own_key, extent, shards, smallest, largest):
    level = 1.0
    for position, parts in shards:
        steps = jax.random.uniform(jax.random.fold_in(jax.random.fold_in(own_key, 6), position), (parts,), jnp.float32, smallest / len(shards), largest / len(shards))
        level = level * jnp.repeat(jnp.exp(steps), extent[position] // parts).reshape((-1,) + (1,) * (len(extent) - 1 - position))
    return level


def split_up(number_of, total, limit, slope):
    weights = [(1 << 20) // math.isqrt(standing ** slope) + 1 for standing in range(2, number_of + 1)]
    spare, holding = total - limit - (number_of - 1), [1] * (number_of - 1)
    while spare > 0:
        free = [i for i in range(number_of - 1) if holding[i] < limit]
        pool, left = sum([weights[i] for i in free]), spare
        for i in free:
            addition = min(limit - holding[i], max(1, left * weights[i] // pool), spare)
            holding[i] = holding[i] + addition
            spare = spare - addition
    return np.array([limit] + holding)


def uneven(rng, number_of, total, most, lean):
    if number_of == 2:
        one = jax.random.randint(rng, (), max(1, total - most), min(most, total - 1) + 1)
        return jnp.stack([one, total - one])
    tallies = jnp.asarray(split_up(number_of, total, most, lean), jnp.int32)
    pairs = (number_of - 1) // 2
    source_of, receiver = tallies[1:1 + 2 * pairs:2], tallies[2:2 + 2 * pairs:2]
    slack = jnp.minimum(source_of - 1, most - receiver)
    shifted = jax.random.randint(jax.random.fold_in(rng, 1), (pairs,), 0, 1 << 20) % (slack + 1)
    tallies = tallies.at[1:1 + 2 * pairs:2].set(source_of - shifted).at[2:2 + 2 * pairs:2].set(receiver + shifted)
    return tallies[jax.random.permutation(jax.random.fold_in(rng, 2), number_of)]


def noise(own_key, extent, deviation, limit, cuts=(), kind=jnp.bfloat16):
    entries = jax.random.normal(own_key, extent, jnp.float32) * deviation
    if len(cuts) > 0:
        entries = level_of(own_key, extent, cuts, -0.22, 0.18) * entries
    return jnp.clip(entries, min=-limit, max=limit).astype(kind)


def setup_inputs(seed: int = 0) -> dict:
    key_list = jax.random.split(jax.random.key(seed), 11)
    return {
        "tokens": draw_tokens(jax.random.fold_in(key_list[10], 71), 0),
        "norm_gain": jnp.clip(1.0 + 0.18 * jax.random.normal(key_list[1], (D,), jnp.float32), 0.1, 1.9),
        "w_query": draw_w_query(jax.random.fold_in(key_list[10], 71), 0),
        "w_key": noise(key_list[3], (D, D), D ** -0.5, 0.21875, ((0, 8),)),
        "w_value": noise(key_list[4], (D, D), (D // 9) ** -0.5, 0.625, ((0, 8),)),
        "w_out": noise(key_list[5], (D, D), D ** -0.5, 0.21875, ((0, 8),)),
        "owner_map": jax.vmap(lambda own: jax.random.permutation(own, N_SHARD))(jax.random.split(key_list[6], N_GROUP)).reshape((N_GROUP, N_SHARD)).astype(jnp.int32),
        "pair_images": draw_pair_images(jax.random.fold_in(key_list[10], 71), 0),
        "pair_count": uneven(key_list[8], DEVICES, PAIRS, PAIR_CAP, 2).astype(jnp.int32),
        "confidence": plant(jax.random.randint(key_list[9], (SLOTS, 2), 1, 9), jax.random.fold_in(key_list[9], 1), 1, 8).astype(jnp.int32),
    }


def layer_norm(values, norm_gain):
    values = values.astype(jnp.float32)
    average = lax.optimization_barrier(jnp.mean(values, axis=-1, keepdims=True))
    centred = values - average
    variance = lax.optimization_barrier(jnp.mean(centred * centred, axis=-1, keepdims=True))
    return (centred * lax.rsqrt(variance + 1e-05) * norm_gain).astype(jnp.bfloat16)

def attend(query_rows, key_rows, value_rows, w_out):
    length = query_rows.shape[0]
    query_heads = query_rows.reshape(length, HEADS, HEAD_DIM).astype(jnp.float32)
    key_heads = key_rows.reshape(length, HEADS, HEAD_DIM).astype(jnp.float32)
    value_heads = value_rows.reshape(length, HEADS, HEAD_DIM).astype(jnp.float32)
    scores = jnp.einsum('qhd,khd->hqk', query_heads, key_heads) * (1.0 / math.sqrt(HEAD_DIM))
    scores = scores - lax.optimization_barrier(jnp.max(scores, axis=-1, keepdims=True))
    expo = jnp.exp(scores)
    attention = (expo / lax.optimization_barrier(jnp.sum(expo, axis=-1, keepdims=True))).astype(jnp.bfloat16)
    attended = jnp.einsum('hqk,khd->qhd', attention.astype(jnp.float32), value_heads)
    attended = attended.reshape(length, HEADS * HEAD_DIM).astype(jnp.bfloat16)
    return jnp.dot(attended, w_out, preferred_element_type=jnp.float32)

def reference(tokens, norm_gain, w_query, w_key, w_value, w_out, owner_map, pair_images, pair_count, confidence):
    normed = layer_norm(tokens, norm_gain)
    flat_rows = normed.reshape(IMAGES * SEQ, D)
    query = jnp.dot(flat_rows, w_query, preferred_element_type=jnp.float32).astype(jnp.bfloat16).reshape(IMAGES, SEQ, D)
    key_all = jnp.dot(flat_rows, w_key, preferred_element_type=jnp.float32).astype(jnp.bfloat16).reshape(IMAGES, SEQ, D)
    value_all = jnp.dot(flat_rows, w_value, preferred_element_type=jnp.float32).astype(jnp.bfloat16).reshape(IMAGES, SEQ, D)
    slot_ids = jnp.arange(SLOTS, dtype=jnp.int32)
    device_ids = slot_ids // PAIR_CAP
    group_ids = device_ids // N_SHARD
    usable = slot_ids % PAIR_CAP < pair_count[device_ids]
    store_first = (group_ids * N_SHARD + owner_map[group_ids, pair_images[:, 0]]).astype(jnp.int32)
    store_second = (group_ids * N_SHARD + owner_map[group_ids, pair_images[:, 1]]).astype(jnp.int32)
    weight_first = jnp.where(usable, confidence[:, 0], 0).astype(jnp.float32)
    weight_second = jnp.where(usable, confidence[:, 1], 0).astype(jnp.float32)

    def advance(carried, element):
        numerator, weight_total = carried
        first, second, first_weight, second_weight = element
        first_out = attend(query[first], key_all[second], value_all[second], w_out)
        second_out = attend(query[second], key_all[first], value_all[first], w_out)
        numerator = numerator.at[first].add(first_weight * first_out)
        numerator = numerator.at[second].add(second_weight * second_out)
        weight_total = weight_total.at[first].add(first_weight)
        weight_total = weight_total.at[second].add(second_weight)
        return ((numerator, weight_total), None)
    start = (jnp.zeros((IMAGES, SEQ, D), jnp.float32), jnp.zeros((IMAGES,), jnp.float32))
    (numerator, weight_total), _ = lax.scan(advance, start, (store_first, store_second, weight_first, weight_second))
    return (numerator / (1.0 + weight_total)[:, None, None]).astype(jnp.bfloat16)
```

```python
import functools
import math

import jax
import jax.numpy as jnp
from jax import lax
from jax.experimental import pallas as pl
from jax.experimental.pallas import tpu as pltpu
from jax.sharding import PartitionSpec as P

HEADS = 12
HEAD_DIM = 64

F32 = jnp.float32
BF16 = jnp.bfloat16
VMEM_LIMIT = 60 * 1024 * 1024
SMEM_SPEC = pl.BlockSpec(memory_space=pltpu.SMEM)
VMEM_SPEC = pl.BlockSpec(memory_space=pltpu.VMEM)
ANY_SPEC = pl.BlockSpec(memory_space=pl.ANY)


def round_up(value, multiple):
    return -(-value // multiple) * multiple


def prepare_kernel(groups, send_weights, *refs):
    where_ref, owner_ref, pairs_ref, count_ref, conf_ref, tokens_ref, gain_ref = refs[:7]
    if send_weights:
        weight_refs = refs[7:10]
        normed_ref, message_ref = refs[10:]
    else:
        normed_ref, table_ref = refs[7:]
    images = owner_ref.shape[1]
    capacity = pairs_ref.shape[0]

    if send_weights:
        rows = weight_refs[0].shape[0]
        table_rows = message_ref.shape[1] - rows
        lanes = message_ref.shape[2]
    else:
        table_rows, lanes = table_ref.shape
    row = lax.broadcasted_iota(jnp.int32, (table_rows, lanes), 0)
    column = lax.broadcasted_iota(jnp.int32, (table_rows, lanes), 1)
    table = jnp.zeros((table_rows, lanes), jnp.int32)
    for p in range(capacity):
        first = owner_ref[0, pairs_ref[p, 0]]
        second = owner_ref[0, pairs_ref[p, 1]]
        listed = p < count_ref[0]
        forward = jnp.where(listed, conf_ref[p, 0], 0)
        backward = jnp.where(listed, conf_ref[p, 1], 0)
        table += jnp.where((row == first) & (column == second), forward, 0)
        table += jnp.where((row == second) & (column == first), backward, 0)
    table = table.astype(F32).astype(BF16)

    if send_weights:
        own = where_ref[0]
        width = weight_refs[0].shape[1] // groups
        for h in range(groups):
            slot = jnp.bitwise_xor(own, h)
            for part, ref in enumerate(weight_refs):
                message_ref[slot, :rows, part * width : (part + 1) * width] = ref[:, h * width : (h + 1) * width]
            message_ref[slot, rows:, :] = table
    else:
        table_ref[...] = table

    values = tokens_ref[...].astype(F32)
    average = jnp.mean(values, axis=-1, keepdims=True)
    centred = values - average
    variance = jnp.mean(centred * centred, axis=-1, keepdims=True)
    normed_ref[...] = (centred * lax.rsqrt(variance + 1e-05) * gain_ref[...]).astype(BF16)


def attention_kernel(cfg, *refs):
    groups, members, heads, low, high, slots, blocks, last = cfg
    refs = list(refs)
    take = lambda count: [refs.pop(0) for _ in range(count)]
    where_ref, slot_ref, block_ref, weight_ref = take(4)
    image_refs = take(slots)
    block_refs = take(blocks)
    first = low < 0
    if not first:
        state_in = take(5)
    if last:
        out_refs = take(groups)
    key_ref, value_ref, query_ref, pair_ref, single_ref = take(5)
    weights, pictures, weight_sem, picture_sem, state_sem = take(5)
    images = groups * members
    own, member = where_ref[0], where_ref[1]
    width = heads * HEAD_DIM
    rows = weights.shape[0] // blocks

    def block_copy(b):
        start = pl.multiple_of(block_ref[b] * rows, 8)
        return pltpu.make_async_copy(
            block_refs[b].at[pl.ds(0, rows), :], weights.at[pl.ds(start, rows), :], weight_sem.at[b]
        )

    def picture_copy(s):
        return pltpu.make_async_copy(image_refs[s], pictures.at[slot_ref[s]], picture_sem.at[s])

    def state_copy(i):
        into = (key_ref, value_ref, query_ref, pair_ref, single_ref)[i]
        return pltpu.make_async_copy(state_in[i], into, state_sem.at[i])

    for b in range(blocks):
        block_copy(b).start()
    for s in range(slots):
        @pl.when(slot_ref[s] >= 0)
        def _(s=s):
            picture_copy(s).start()
    if not first:
        for i in range(5):
            state_copy(i).start()
    for b in range(blocks):
        block_copy(b).wait()
    for s in range(slots):
        @pl.when(slot_ref[s] >= 0)
        def _(s=s):
            picture_copy(s).wait()
    if not first:
        for i in range(5):
            state_copy(i).wait()

    def distance(image):
        return jnp.abs(image // members - own)

    if first:
        pair_ref[...] = jnp.zeros_like(pair_ref)
        single_ref[...] = jnp.zeros_like(single_ref)

    def project(image, carry):
        away = distance(image)

        @pl.when((away > low) & (away <= high))
        def _():
            rows_in = pictures[image]
            key = jnp.dot(rows_in, weights[:, width : 2 * width], preferred_element_type=F32)
            key_ref[image] = key.astype(BF16)
            value = jnp.dot(rows_in, weights[:, 2 * width : 3 * width], preferred_element_type=F32)
            value_ref[image] = value.astype(BF16).T

            @pl.when(image % members == member)
            def _():
                query = jnp.dot(rows_in, weights[:, :width], preferred_element_type=F32).astype(BF16)
                flipped = query.T
                row = lax.broadcasted_iota(jnp.int32, flipped.shape, 0) // HEAD_DIM
                length = flipped.shape[1]
                for h in range(heads):
                    query_ref[image // members, :, h * length : (h + 1) * length] = jnp.where(
                        row == h, flipped, jnp.zeros_like(flipped)
                    )

        return carry

    lax.fori_loop(0, images, project, 0)

    scale = math.log2(math.e) / math.sqrt(HEAD_DIM)

    def direction(number, carry):
        query_group, target = number // images, number % images
        amount = weight_ref[query_group * members + member, target]
        away = jnp.maximum(jnp.abs(query_group - own), distance(target))

        @pl.when((amount > 0) & (away > low) & (away <= high))
        def _():
            scores = jnp.dot(key_ref[target], query_ref[query_group], preferred_element_type=F32)
            largest = jnp.max(scores, axis=0, keepdims=True)
            expo = jnp.exp2((scores - largest) * scale)
            total = jnp.sum(expo, axis=0, keepdims=True)
            attention = (expo * (1.0 / total)).astype(BF16)
            length = scores.shape[1] // heads
            values = value_ref[target]
            pairs = heads // 2
            for j in range(pairs):
                part = jnp.dot(
                    values[2 * j * HEAD_DIM : 2 * (j + 1) * HEAD_DIM],
                    attention[:, 2 * j * length : 2 * (j + 1) * length],
                    preferred_element_type=F32,
                )
                pair_ref[query_group, j] += amount * part
            if heads % 2:
                part = jnp.dot(
                    values[(heads - 1) * HEAD_DIM :],
                    attention[:, (heads - 1) * length :],
                    preferred_element_type=F32,
                )
                single_ref[query_group] += amount * part

        return carry

    lax.fori_loop(0, groups * images, direction, 0)

    if last:
        for k in range(groups):
            query_group = jnp.bitwise_xor(own, k)
            total = jnp.float32(1.0)
            for target in range(images):
                total += weight_ref[query_group * members + member, target]
            pieces = []
            length = single_ref.shape[2]
            for h in range(heads):
                if h == heads - 1 and heads % 2:
                    piece = single_ref[query_group]
                else:
                    at = h % 2
                    piece = pair_ref[
                        query_group, h // 2, at * HEAD_DIM : (at + 1) * HEAD_DIM, at * length : (at + 1) * length
                    ]
                pieces.append(piece)
            whole = (jnp.concatenate(pieces, axis=0) / total).T.astype(BF16)
            half = length // 2
            out_refs[k][:, :width] = whole[:half]
            out_refs[k][:, width:] = whole[half:]


def output_kernel(cfg, *refs):
    groups, blocks = cfg
    refs = list(refs)
    take = lambda count: [refs.pop(0) for _ in range(count)]
    where_ref, block_ref = take(2)
    part_refs = take(groups)
    block_refs = take(blocks)
    (out_ref,) = take(1)
    weights, sem = take(2)
    rows = weights.shape[0] // blocks

    def block_copy(b):
        start = pl.multiple_of(block_ref[b] * rows, 8)
        return pltpu.make_async_copy(block_refs[b], weights.at[pl.ds(start, rows), :], sem.at[b])

    for b in range(blocks):
        block_copy(b).start()
    for b in range(blocks):
        block_copy(b).wait()
    total = jnp.zeros(out_ref.shape, F32)
    for k in range(groups):
        source = jnp.bitwise_xor(where_ref[0], k)
        width = part_refs[k].shape[1] // 2
        part = jnp.concatenate([part_refs[k][:, :width], part_refs[k][:, width:]], axis=0)
        start = pl.multiple_of(source * width, 8)
        total += jnp.dot(part, weights[pl.ds(start, width), :], preferred_element_type=F32)
    out_ref[...] = total.astype(BF16)


def params():
    return pltpu.CompilerParams(vmem_limit_bytes=VMEM_LIMIT)


def shards(devices, tokens, norm_gain, w_query, w_key, w_value, w_out, owner_map, pair_images, pair_count, confidence):
    groups = math.gcd(HEADS & -HEADS, devices)
    members = devices // groups
    heads = HEADS // groups
    width = heads * HEAD_DIM
    length, features = tokens.shape[1:]
    rows = w_query.shape[0]
    position = lax.axis_index("shard")
    own, member = position // members, position % members
    where = jnp.stack([own, member]).astype(jnp.int32)
    relayed = members == 2
    table_rows = round_up(devices, 16)
    gain = norm_gain.reshape(1, features)
    small = (where, owner_map, pair_images, pair_count, confidence)

    normed_shape = jax.ShapeDtypeStruct((length, features), BF16)
    if relayed:
        normed, message = pl.pallas_call(
            functools.partial(prepare_kernel, groups, True),
            out_shape=(normed_shape, jax.ShapeDtypeStruct((groups, rows + table_rows, 3 * width), BF16)),
            in_specs=[SMEM_SPEC] * 5 + [VMEM_SPEC] * 5,
            out_specs=(VMEM_SPEC, VMEM_SPEC),
            compiler_params=params(),
            name="prepare",
        )(*small, tokens[0], gain, w_query, w_key, w_value)
    else:
        normed, table = pl.pallas_call(
            functools.partial(prepare_kernel, groups, False),
            out_shape=(normed_shape, jax.ShapeDtypeStruct((table_rows, 128), BF16)),
            in_specs=[SMEM_SPEC] * 5 + [VMEM_SPEC] * 2,
            out_specs=(VMEM_SPEC, VMEM_SPEC),
            compiler_params=params(),
            name="prepare",
        )(*small, tokens[0], gain)

    across = lambda k: [(i, i ^ (k * members)) for i in range(devices)]
    stage_images, stage_slots = [], []
    if relayed:
        swap = lambda x: lax.ppermute(x, "shard", [(i, i ^ 1) for i in range(devices)])
        mine = [message[0]] + [lax.ppermute(message[k], "shard", across(k)) for k in range(1, groups)]
        others = [swap(x) for x in mine]
        weight_blocks = mine + others
        block_at = jnp.stack(
            [(own ^ k) * 2 + member for k in range(groups)] + [(own ^ k) * 2 + 1 - member for k in range(groups)]
        ).astype(jnp.int32)
        table = sum(x[rows : rows + devices, :devices].astype(F32) for x in weight_blocks)

        ahead = jnp.where(member == 0, -1, 1)
        index = lambda place, who: jnp.where((place >= 0) & (place < groups), place * 2 + who, -1)
        own_a, own_b = normed, swap(normed)
        images, slots = [own_a, own_b], [own * 2 + member, own * 2 + 1 - member]
        a, b = own_a, own_b
        for k in range(1, groups):
            pairs = [(2 * z, 2 * z + 2) for z in range(k - 1, groups - 1)]
            pairs += [(2 * z + 1, 2 * z - 1) for z in range(1, groups - k + 1)]
            a, b = lax.ppermute(a, "shard", pairs), lax.ppermute(b, "shard", pairs)
            images += [a, b, swap(a), swap(b)]
            slots += [
                index(own + k * ahead, member),
                index(own + k * ahead, 1 - member),
                index(own - k * ahead, 1 - member),
                index(own - k * ahead, member),
            ]
            if k == groups - 2 or k == groups - 1:
                stage_images.append(images)
                stage_slots.append(slots)
                images, slots = [], []
        wo = [w_out] + [lax.ppermute(w_out, "shard", across(k)) for k in range(1, groups)]
        out_blocks = wo + [swap(x) for x in wo]
        out_at = block_at
    else:
        gather = lambda x: lax.all_gather(x, "shard", axis=0, tiled=True)
        columns = lambda w: lax.dynamic_slice_in_dim(gather(w), own * width, width, 1)
        weight_blocks = [jnp.concatenate([columns(w) for w in (w_query, w_key, w_value)], axis=1)]
        block_at = jnp.zeros((1,), jnp.int32)
        tables = gather(table[None])
        table = jnp.sum(tables[:, :devices, :devices].astype(F32), axis=0)
        every = gather(normed[None])
        stage_images.append([every[i] for i in range(devices)])
        stage_slots.append([jnp.int32(i) for i in range(devices)])
        out_blocks = [gather(w_out)]
        out_at = jnp.zeros((1,), jnp.int32)

    state_shapes = (
        jax.ShapeDtypeStruct((devices, length, width), BF16),
        jax.ShapeDtypeStruct((devices, width, length), BF16),
        jax.ShapeDtypeStruct((groups, width, heads * length), BF16),
        jax.ShapeDtypeStruct((groups, max(heads // 2, 1), 2 * HEAD_DIM, 2 * length), F32),
        jax.ShapeDtypeStruct((groups, HEAD_DIM, length), F32),
    )
    part_shapes = tuple(jax.ShapeDtypeStruct((length // 2, 2 * width), BF16) for _ in range(groups))
    state = ()
    stages = len(stage_images)
    bounds = [-1] + [groups - 2 if (relayed and s == 0) else groups for s in range(stages)]
    for s in range(stages):
        first, last = s == 0, s == stages - 1
        images = stage_images[s]
        slots = jnp.stack(stage_slots[s]).astype(jnp.int32)
        cfg = (groups, members, heads, bounds[s], bounds[s + 1], len(images), len(weight_blocks), last)
        scratch = [
            pltpu.VMEM((features, 3 * width), BF16),
            pltpu.VMEM((devices, length, features), BF16),
            pltpu.SemaphoreType.DMA((len(weight_blocks),)),
            pltpu.SemaphoreType.DMA((len(images),)),
            pltpu.SemaphoreType.DMA((5,)),
        ]
        if last:
            scratch = [pltpu.VMEM(x.shape, x.dtype) for x in state_shapes] + scratch
        shapes = part_shapes if last else state_shapes
        state = pl.pallas_call(
            functools.partial(attention_kernel, cfg),
            out_shape=shapes,
            in_specs=[SMEM_SPEC] * 4 + [ANY_SPEC] * (len(images) + len(weight_blocks) + len(state)),
            out_specs=(VMEM_SPEC,) * len(shapes),
            scratch_shapes=scratch,
            compiler_params=params(),
            name=f"attention_{s}",
        )(where, slots, block_at, table, *images, *weight_blocks, *state)

    parts = [state[0]] + [lax.ppermute(state[k], "shard", across(k)) for k in range(1, groups)]
    out = pl.pallas_call(
        functools.partial(output_kernel, (groups, len(out_blocks))),
        out_shape=jax.ShapeDtypeStruct((length, features), BF16),
        in_specs=[SMEM_SPEC] * 2 + [VMEM_SPEC] * groups + [ANY_SPEC] * len(out_blocks),
        out_specs=VMEM_SPEC,
        scratch_shapes=[pltpu.VMEM((features, features), BF16), pltpu.SemaphoreType.DMA((len(out_blocks),))],
        compiler_params=params(),
        name="output",
    )(where, out_at, *parts, *out_blocks)
    return out[None]


def solution(mesh):
    in_specs = (
        P(("group", "shard"), None, None),
        P(),
        P("shard", None),
        P("shard", None),
        P("shard", None),
        P("shard", None),
        P("group", None),
        P(("group", "shard"), None),
        P(("group", "shard")),
        P(("group", "shard"), None),
    )
    out_specs = P(("group", "shard"), None, None)
    return jax.shard_map(
        functools.partial(shards, mesh.shape["shard"]),
        mesh=mesh,
        in_specs=in_specs,
        out_specs=out_specs,
        check_vma=False,
    )
```

```python
import functools
import math

import jax
import jax.numpy as jnp
from jax import lax
from jax.experimental import pallas as pl
from jax.experimental.pallas import tpu as pltpu
from jax.sharding import PartitionSpec as P

HEADS = 12
HEAD_DIM = 64
TOGETHER = 4

F32 = jnp.float32
BF16 = jnp.bfloat16
SMEM_SPEC = pl.BlockSpec(memory_space=pltpu.SMEM)
VMEM_SPEC = pl.BlockSpec(memory_space=pltpu.VMEM)


def round_up(value, multiple):
    return -(-value // multiple) * multiple


def struct(shape, dtype=BF16):
    return jax.ShapeDtypeStruct(shape, dtype)


def call(kernel, name, out_shape, smem, vmem, scratch=(), megabytes=16, cost=None):
    many = isinstance(out_shape, (tuple, list))
    return pl.pallas_call(
        kernel,
        out_shape=tuple(out_shape) if many else out_shape,
        in_specs=[SMEM_SPEC] * len(smem) + [VMEM_SPEC] * len(vmem),
        out_specs=(VMEM_SPEC,) * len(out_shape) if many else VMEM_SPEC,
        scratch_shapes=list(scratch),
        compiler_params=pltpu.CompilerParams(vmem_limit_bytes=megabytes * 1024 * 1024),
        cost_estimate=cost,
        name=name,
    )(*smem, *vmem)


def places(members):
    position = lax.axis_index("shard")
    return position // members, position % members


def direction_table(owner_ref, pairs_ref, count_ref, conf_ref, shape):
    row = lax.broadcasted_iota(jnp.int32, shape, 0)
    column = lax.broadcasted_iota(jnp.int32, shape, 1)
    table = jnp.zeros(shape, jnp.int32)
    for p in range(pairs_ref.shape[1]):
        first = owner_ref[0, pairs_ref[0, p]]
        second = owner_ref[0, pairs_ref[1, p]]
        listed = p < count_ref[0]
        forward = jnp.where(listed, conf_ref[0, p], 0)
        backward = jnp.where(listed, conf_ref[1, p], 0)
        table += jnp.where((row == first) & (column == second), forward, 0)
        table += jnp.where((row == second) & (column == first), backward, 0)
    return table.astype(F32)


def table_kernel(owner_ref, pairs_ref, count_ref, conf_ref, table_ref):
    table_ref[...] = direction_table(owner_ref, pairs_ref, count_ref, conf_ref, table_ref.shape).astype(BF16)


def message_kernel(cfg, *refs):
    groups, members, sharers, table_rows = cfg
    owner_ref, pairs_ref, count_ref, conf_ref, query_ref, key_ref, value_ref, out_ref = refs[:8]
    own_ref = refs[8]
    message_refs = refs[9 : 8 + groups]
    wide = refs[8 + groups]
    own, _ = places(members)
    rows, features = query_ref.shape
    width = features // groups
    part = rows // sharers
    start = pl.multiple_of(lax.axis_index("group") * part, 8)
    out_lane = message_refs[0].shape[1] - out_ref.shape[1]
    for i, ref in enumerate((key_ref, value_ref, query_ref, out_ref)):
        wide[i] = ref[...].astype(F32)
    table = direction_table(owner_ref, pairs_ref, count_ref, conf_ref, (table_rows, 128)).astype(BF16)
    for h in range(groups):
        cut = slice(h * width, (h + 1) * width)

        @pl.when(own == h)
        def _(cut=cut):
            for i, ref in enumerate((key_ref, value_ref, query_ref)):
                own_ref[:rows, i * width : (i + 1) * width] = ref[:, cut]

        for k in range(1, groups):

            @pl.when(own == h ^ k)
            def _(k=k, cut=cut):
                for i in range(3):
                    message_refs[k - 1][:part, i * width : (i + 1) * width] = wide[i, pl.ds(start, part), cut].astype(BF16)

    own_ref[rows:, :128] = table
    for ref in message_refs:
        ref[:part, out_lane:] = wide[3, pl.ds(start, part), :].astype(BF16)
        ref[part:, :128] = table


def norm_kernel(tokens_ref, gain_ref, normed_ref):
    values = tokens_ref[...].astype(F32)
    average = jnp.mean(values, axis=-1, keepdims=True)
    centred = values - average
    variance = jnp.mean(centred * centred, axis=-1, keepdims=True)
    gain = gain_ref[...].reshape(1, gain_ref.shape[0])
    normed_ref[...] = (centred * lax.rsqrt(variance + 1e-05) * gain).astype(BF16)


def gathered_kernel(cfg, own_ref, *refs):
    groups, rows, sharers = cfg
    shared_refs = refs[:sharers]
    table_refs = refs[sharers:-2]
    block_ref, wide = refs[-2:]
    part = rows // sharers
    mine = lax.axis_index("group")
    block_ref[:rows] = own_ref[:rows]
    for j in range(sharers):
        for k in range(1, groups):
            start = pl.multiple_of((k - 1) * rows + jnp.bitwise_xor(mine, j) * part, 8)
            wide[pl.ds(start, part), :] = shared_refs[j][(k - 1) * part : k * part, :].astype(F32)
    block_ref[rows : groups * rows] = wide[...].astype(BF16)
    if table_refs:
        size = table_refs[0].shape[0] - part
        at = groups * rows
        block_ref[at : at + size, :128] = own_ref[rows:, :128]
        for k in range(1, groups):
            at += size
            block_ref[at : at + size, :128] = table_refs[k - 1][part:, :128]


def joined_kernel(cfg, mine_ref, other_ref, whole_ref):
    groups, members, rows = cfg
    own, member = places(members)
    for k in range(groups):
        source = jnp.bitwise_xor(own, k) * members
        for ref, who in ((mine_ref, member), (other_ref, 1 - member)):
            start = pl.multiple_of((source + who) * rows, 16)
            whole_ref[pl.ds(start, rows), :] = ref[k * rows : (k + 1) * rows, :]


def attention_kernel(cfg, *refs):
    groups, members, heads, low, high, slots, last = cfg
    refs = list(refs)
    take = lambda count: [refs.pop(0) for _ in range(count)]
    (table_ref, weights) = take(2)
    image_refs = take(len(slots))
    first = low < 0
    state_in = [] if first else take(5)
    out_refs = take(groups) if last else []
    key_ref, value_ref, query_ref, pair_ref, single_ref = take(5)
    pictures, list_ref = take(2)
    images = groups * members
    own, member = places(members)
    width = heads * HEAD_DIM
    length = image_refs[0].shape[0]
    ahead = 2 * member - 1

    for ref, (step, flip) in zip(image_refs, slots):
        if step is None:
            pictures[flip // members, (flip % members) * length : (flip % members + 1) * length, :] = ref[...]
            continue
        place = own + step * ahead
        who = jnp.bitwise_xor(member, flip)

        @pl.when((place >= 0) & (place < groups))
        def _(ref=ref, place=place, who=who):
            pictures[place, pl.ds(pl.multiple_of(who * length, 16), length), :] = ref[...]

    if first:
        pair_ref[...] = jnp.zeros_like(pair_ref)
        single_ref[...] = jnp.zeros_like(single_ref)
    else:
        for new, old in zip((key_ref, value_ref, query_ref, pair_ref, single_ref), state_in):
            new[...] = old[...]

    def listed(number, count):
        place, target = number // images, number % images
        away = jnp.maximum(jnp.abs(place - own), jnp.abs(target // members - own))
        amount = table_ref[place * members + member, target]
        list_ref[count] = number
        return count + ((amount > 0) & (away > low) & (away <= high)).astype(jnp.int32)

    count = jnp.int32(0)
    for number in range(groups * images):
        count = listed(number, count)

    def project(place, carry):
        away = jnp.abs(place - own)

        @pl.when((away > low) & (away <= high))
        def _():
            both = jnp.dot(pictures[place], weights[:, : 2 * width], preferred_element_type=F32).astype(BF16)
            aligned = width // 128 * 128
            for who in range(members):
                rows = both[who * length : (who + 1) * length]
                key_ref[place * members + who] = rows[:, :width]
                value_ref[place * members + who] = rows[:, aligned:].T[width - aligned :]
            rows = pictures[place, pl.ds(pl.multiple_of(member * length, 16), length), :]
            query = jnp.dot(rows, weights[:, 2 * width : 3 * width], preferred_element_type=F32).astype(BF16)
            flipped = query.T
            head = lax.broadcasted_iota(jnp.int32, flipped.shape, 0) // HEAD_DIM
            for h in range(heads):
                query_ref[place, :, h * length : (h + 1) * length] = jnp.where(
                    head == h, flipped, jnp.zeros_like(flipped)
                )

        return carry

    lax.fori_loop(0, groups, project, 0)

    scale = math.log2(math.e) / math.sqrt(HEAD_DIM)
    paired = heads // 2

    def block(number, carry):
        entries = []
        for u in range(TOGETHER):
            at = number * TOGETHER + u
            there = at < count
            entry = jnp.where(there, list_ref[jnp.where(there, at, 0)], list_ref[0])
            place, target = entry // images, entry % images
            amount = jnp.where(there, table_ref[place * members + member, target], 0.0)
            entries.append((place, target, amount))
        scores = [jnp.dot(key_ref[t], query_ref[s], preferred_element_type=F32) for s, t, _ in entries]
        expos, factors = [], []
        for each, (_, _, amount) in zip(scores, entries):
            largest = jnp.max(each, axis=0, keepdims=True)
            expo = jnp.exp2((each - largest) * scale)
            total = jnp.sum(expo, axis=0, keepdims=True)
            expos.append(expo.astype(BF16))
            factors.append(amount / total)
        parts = []
        for (_, target, _), expo, factor in zip(entries, expos, factors):
            for j in range(paired):
                rows, lanes = slice(2 * j * HEAD_DIM, 2 * (j + 1) * HEAD_DIM), slice(2 * j * length, 2 * (j + 1) * length)
                part = jnp.dot(value_ref[target, rows, :], expo[:, lanes], preferred_element_type=F32)
                parts.append(part * factor[:, lanes])
            if heads % 2:
                rows, lanes = slice((heads - 1) * HEAD_DIM, None), slice((heads - 1) * length, None)
                part = jnp.dot(value_ref[target, rows, :], expo[:, lanes], preferred_element_type=F32)
                parts.append(part * factor[:, lanes])
        for place, _, _ in entries:
            for j in range(paired):
                pair_ref[place, j] += parts.pop(0)
            if heads % 2:
                single_ref[place] += parts.pop(0)
        return carry

    lax.fori_loop(0, (count + TOGETHER - 1) // TOGETHER, block, 0)

    if last:
        for k in range(groups):
            place = jnp.bitwise_xor(own, k)
            total = jnp.float32(1.0)
            for target in range(images):
                total += table_ref[place * members + member, target]
            pieces = []
            for h in range(heads):
                if h == heads - 1 and heads % 2:
                    pieces.append(single_ref[place])
                else:
                    at = h % 2
                    pieces.append(
                        pair_ref[place, h // 2, at * HEAD_DIM : (at + 1) * HEAD_DIM, at * length : (at + 1) * length]
                    )
            whole = (jnp.concatenate(pieces, axis=0) / total).T.astype(BF16)
            half = length // 2
            out_refs[k][:, :width] = whole[:half]
            out_refs[k][:, width:] = whole[half:]


def output_kernel(cfg, *refs):
    groups, members = cfg
    weights = refs[0]
    part_refs = refs[1 : 1 + groups]
    out_ref, gathered = refs[1 + groups :]
    own, _ = places(members)
    half = part_refs[0].shape[0]
    width = part_refs[0].shape[1] // 2
    for k in range(groups):
        source = jnp.bitwise_xor(own, k)
        gathered[source, :half] = part_refs[k][:, :width]
        gathered[source, half:] = part_refs[k][:, width:]
    whole = jnp.concatenate([gathered[h] for h in range(groups)], axis=1)
    out_ref[...] = jnp.dot(whole, weights[...], preferred_element_type=F32).astype(BF16)


def shards(mesh_shape, tokens, norm_gain, w_query, w_key, w_value, w_out, owner_map, pair_images, pair_count, confidence):
    devices, sharers = mesh_shape["shard"], mesh_shape["group"]
    groups = math.gcd(HEADS & -HEADS, devices)
    members = devices // groups
    heads = HEADS // groups
    width = heads * HEAD_DIM
    length, features = tokens.shape[1:]
    rows = w_query.shape[0]
    small = (owner_map, pair_images.T, pair_count, confidence.T)
    relayed = members == 2 and sharers & (sharers - 1) == 0 and rows % (8 * sharers) == 0 and rows % 16 == 0
    across = lambda k: [(i, i ^ (k * members)) for i in range(devices)]
    exchange = lambda x, k: lax.ppermute(x, "shard", across(k))

    normed = functools.partial(call, norm_kernel, "norm", struct((length, features)), (), (tokens[0], norm_gain))
    stage_images, stage_slots = [], []
    if relayed:
        part = rows // sharers
        table_rows = round_up(devices, 8)
        lanes = 3 * width
        wide_lanes = round_up(lanes, 128) + features
        swap = lambda x: lax.ppermute(x, "shard", [(i, i ^ 1) for i in range(devices)])
        share = lambda x, j: lax.ppermute(
            x, ("group", "shard"), [(g * devices + i, (g ^ j) * devices + i) for g in range(sharers) for i in range(devices)]
        )
        own_block, *messages = call(
            functools.partial(message_kernel, (groups, members, sharers, table_rows)),
            "message",
            [struct((rows + table_rows, lanes))] + [struct((part + table_rows, wide_lanes))] * (groups - 1),
            small,
            (w_query, w_key, w_value, w_out),
            [pltpu.VMEM((4, rows, features), F32)],
        )
        messages = [exchange(messages[k - 1], k) for k in range(1, groups)]
        normed = normed()

        own_a, own_b = normed, swap(normed)
        images, slots = [own_a, own_b], [(0, 0), (0, 1)]
        a, b = own_a, own_b
        for k in range(1, groups):
            pairs = [(2 * z, 2 * z + 2) for z in range(k - 1, groups - 1)]
            pairs += [(2 * z + 1, 2 * z - 1) for z in range(1, groups - k + 1)]
            a, b = lax.ppermute(a, "shard", pairs), lax.ppermute(b, "shard", pairs)
            images += [a, b, swap(a), swap(b)]
            slots += [(k, 0), (k, 1), (-k, 1), (-k, 0)]
            if k == groups - 2 or k == groups - 1:
                stage_images.append(images)
                stage_slots.append(tuple(slots))
                images, slots = [], []

        def collect(own, mine, tables, columns, name):
            shared = [mine] + [share(mine, j) for j in range(1, sharers)]
            block = call(
                functools.partial(gathered_kernel, (groups, rows, sharers)),
                name,
                struct((groups * (rows + (table_rows if tables else 0)), columns)),
                (),
                (own, *shared, *tables),
                [pltpu.VMEM(((groups - 1) * rows, columns), F32)],
            )
            return block, swap(block)

        mine, other = collect(
            own_block, jnp.concatenate([x[:part, :lanes] for x in messages], axis=0), messages, lanes, "gathered"
        )
        join = functools.partial(joined_kernel, (groups, members, rows))
        weights = call(join, "joined", struct((features, lanes)), (), (mine, other))
        table = sum(
            x[at : at + devices, :devices].astype(F32)
            for x in (mine, other)
            for at in range(groups * rows, groups * (rows + table_rows), table_rows)
        )
        out_mine = jnp.concatenate([x[:part, wide_lanes - features :] for x in messages], axis=0)
        out_weights = lambda: call(
            join, "out_joined", struct((features, features)), (), collect(w_out, out_mine, (), features, "out_gathered")
        )
    else:
        gather = lambda x: lax.all_gather(x, "shard", axis=0, tiled=True)
        own = lax.axis_index("shard") // members
        columns = lambda w: lax.dynamic_slice_in_dim(gather(w), own * width, width, 1)
        weights = jnp.concatenate([columns(w) for w in (w_key, w_value, w_query)], axis=1)
        table = call(table_kernel, "table", struct((round_up(devices, 16), 128)), small, ())
        table = jnp.sum(gather(table[None])[:, :devices, :devices].astype(F32), axis=0)
        every = gather(normed()[None])
        stage_images.append([every[i] for i in range(devices)])
        stage_slots.append(tuple((None, i) for i in range(devices)))
        out_weights = lambda: gather(w_out)

    state_shapes = (
        struct((devices, length, width)),
        struct((devices, width, length)),
        struct((groups, width, heads * length)),
        struct((groups, max(heads // 2, 1), 2 * HEAD_DIM, 2 * length), F32),
        struct((groups, HEAD_DIM, length), F32),
    )
    part_shapes = tuple(struct((length // 2, 2 * width)) for _ in range(groups))
    state = ()
    stages = len(stage_images)
    bounds = [-1] + [groups - 2 if s < stages - 1 else groups for s in range(stages)]
    for s in range(stages):
        last = s == stages - 1
        cfg = (groups, members, heads, bounds[s], bounds[s + 1], stage_slots[s], last)
        scratch = [pltpu.VMEM((groups, members * length, features), BF16), pltpu.SMEM((groups * devices + 1,), jnp.int32)]
        if last:
            scratch = [pltpu.VMEM(x.shape, x.dtype) for x in state_shapes] + scratch
        state = call(
            functools.partial(attention_kernel, cfg),
            f"attention_{s}",
            part_shapes if last else state_shapes,
            (table,),
            (weights, *stage_images[s], *state),
            scratch,
            megabytes=24 if relayed else 60,
        )

    parts = [state[0]] + [exchange(state[k], k) for k in range(1, groups)]
    out = call(
        functools.partial(output_kernel, (groups, members)),
        "output",
        struct((length, features)),
        (),
        (out_weights(), *parts),
        [pltpu.VMEM((groups, length, width), BF16)],
    )
    return out[None]


def solution(mesh):
    in_specs = (
        P(("group", "shard"), None, None),
        P(),
        P("shard", None),
        P("shard", None),
        P("shard", None),
        P("shard", None),
        P("group", None),
        P(("group", "shard"), None),
        P(("group", "shard")),
        P(("group", "shard"), None),
    )
    out_specs = P(("group", "shard"), None, None)
    return jax.shard_map(
        functools.partial(shards, dict(mesh.shape)),
        mesh=mesh,
        in_specs=in_specs,
        out_specs=out_specs,
        check_vma=False,
    )
```

```python
import functools
import math

import jax
import jax.numpy as jnp
from jax import lax
from jax.experimental import pallas as pl
from jax.experimental.pallas import tpu as pltpu
from jax.sharding import PartitionSpec as P


HEADS = 12
HEAD_DIM = 64
TOGETHER = 4

F32 = jnp.float32
BF16 = jnp.bfloat16
HBM_SPEC = pl.BlockSpec(memory_space=pltpu.HBM)
SMEM_SPEC = pl.BlockSpec(memory_space=pltpu.SMEM)
VMEM_SPEC = pl.BlockSpec(memory_space=pltpu.VMEM)


def round_up(value, multiple):
    return -(-value // multiple) * multiple


def struct(shape, dtype=BF16):
    return jax.ShapeDtypeStruct(shape, dtype)


def call(kernel, out_shape, smem, vmem, scratch=(), megabytes=16, whole=()):
    many = isinstance(out_shape, (tuple, list))
    return pl.pallas_call(
        kernel,
        out_shape=tuple(out_shape) if many else out_shape,
        in_specs=[SMEM_SPEC] * len(smem) + [VMEM_SPEC] * len(vmem) + [HBM_SPEC] * len(whole),
        out_specs=(VMEM_SPEC,) * len(out_shape) if many else VMEM_SPEC,
        scratch_shapes=list(scratch),
        compiler_params=pltpu.CompilerParams(vmem_limit_bytes=megabytes * 1024 * 1024),
    )(*smem, *vmem, *whole)


def places(members):
    position = lax.axis_index("shard")
    return position // members, position % members


def direction_table(owner_ref, pairs_ref, count_ref, conf_ref, shape):
    row = lax.broadcasted_iota(jnp.int32, shape, 0)
    column = lax.broadcasted_iota(jnp.int32, shape, 1)
    table = jnp.zeros(shape, jnp.int32)
    for p in range(pairs_ref.shape[1]):
        first = owner_ref[0, pairs_ref[0, p]]
        second = owner_ref[0, pairs_ref[1, p]]
        listed = p < count_ref[0]
        forward = jnp.where(listed, conf_ref[0, p], 0)
        backward = jnp.where(listed, conf_ref[1, p], 0)
        table += jnp.where((row == first) & (column == second), forward, 0)
        table += jnp.where((row == second) & (column == first), backward, 0)
    return table.astype(F32)


def table_kernel(owner_ref, pairs_ref, count_ref, conf_ref, table_ref):
    table_ref[...] = direction_table(owner_ref, pairs_ref, count_ref, conf_ref, table_ref.shape).astype(BF16)


def message_kernel(cfg, *refs):
    groups, members, sharers = cfg
    sources, refs = refs[:10], refs[10:]
    normed_ref, own_ref, message_refs, refs = refs[0], refs[1], refs[2 : 1 + groups], refs[1 + groups :]
    copied, wide, sem = refs[:10], refs[10], refs[11]
    owner_ref, pairs_ref, count_ref, conf_ref, query_ref, key_ref, value_ref, out_ref, tokens_ref, gain_ref = copied
    copies = [pltpu.make_async_copy(source, into, sem.at[i]) for i, (source, into) in enumerate(zip(sources, copied))]
    for each in copies:
        each.start()
    own, _ = places(members)
    rows, features = query_ref.shape
    width = features // groups
    part = rows // sharers
    start = pl.multiple_of(lax.axis_index("group") * part, 8)
    lanes = own_ref.shape[1]
    for each in copies:
        each.wait()
    for i, ref in enumerate((key_ref, value_ref, query_ref, out_ref)):
        wide[i] = ref[...].astype(F32)
    for h in range(groups):
        cut = slice(h * width, (h + 1) * width)

        @pl.when(own == h)
        def _(cut=cut):
            for i, ref in enumerate((key_ref, value_ref, query_ref)):
                own_ref[:, i * width : (i + 1) * width] = ref[:, cut]

        for k in range(1, groups):

            @pl.when(own == h ^ k)
            def _(k=k, cut=cut):
                for i in range(3):
                    message_refs[k - 1][:, i * width : (i + 1) * width] = wide[i, pl.ds(start, part), cut].astype(BF16)

    images = groups * members
    table = direction_table(owner_ref, pairs_ref, count_ref, conf_ref, (images, lanes - 3 * width)).astype(BF16)
    own_ref[:images, 3 * width :] = table
    for ref in message_refs:
        ref[:, lanes:] = wide[3, pl.ds(start, part), :].astype(BF16)
        ref[:images, 3 * width : lanes] = table
    normed_ref[...] = layer_norm(tokens_ref[...], gain_ref[...])


def layer_norm(tokens, gain):
    values = tokens.astype(F32)
    average = jnp.mean(values, axis=-1, keepdims=True)
    centred = values - average
    variance = jnp.mean(centred * centred, axis=-1, keepdims=True)
    return (centred * lax.rsqrt(variance + 1e-05) * gain.reshape(1, gain.shape[0])).astype(BF16)


def norm_kernel(tokens_ref, gain_ref, normed_ref):
    normed_ref[...] = layer_norm(tokens_ref[...], gain_ref[...])


def packed_kernel(*refs):
    message_refs, packed_ref = refs[:-1], refs[-1]
    part = message_refs[0].shape[0]
    for k, ref in enumerate(message_refs):
        packed_ref[k * part : (k + 1) * part] = ref[...]


def gathered_kernel(cfg, own_ref, out_ref, *refs):
    groups, rows, sharers, images, spare = cfg
    shared_refs = refs[:sharers]
    in_block, out_block, wide = refs[sharers:]
    part = rows // sharers
    lanes = in_block.shape[1]
    mine = lax.axis_index("group")
    in_block[:rows] = own_ref[...]
    out_block[:rows] = out_ref[...]
    for j in range(sharers):
        for k in range(1, groups):
            start = pl.multiple_of((k - 1) * rows + jnp.bitwise_xor(mine, j) * part, 8)
            wide[pl.ds(start, part), :] = shared_refs[j][(k - 1) * part : k * part, :].astype(F32)
    in_block[rows:] = wide[:, :lanes].astype(BF16)
    out_block[rows:] = wide[:, lanes:].astype(BF16)
    for k in range(1, groups):
        in_block[k * rows : k * rows + images, spare:] = shared_refs[0][(k - 1) * part : (k - 1) * part + images, spare:lanes]


def joined_kernel(cfg, mine_ref, other_ref, whole_ref):
    groups, members, rows = cfg
    own, member = places(members)
    for k in range(groups):
        source = jnp.bitwise_xor(own, k) * members
        for ref, who in ((mine_ref, member), (other_ref, 1 - member)):
            start = pl.multiple_of((source + who) * rows, 16)
            whole_ref[pl.ds(start, rows), :] = ref[k * rows : (k + 1) * rows, :]


def attention_kernel(cfg, *refs):
    groups, members, heads, low, high, slots, last = cfg
    refs = list(refs)
    take = lambda count: [refs.pop(0) for _ in range(count)]
    table_ref, weights = take(2)
    image_refs = take(len(slots))
    first = low < 0
    state_in = [] if first else take(5)
    out_refs = take(groups) if last else []
    key_ref, value_ref, query_ref, pair_ref, single_ref = take(5)
    pictures, list_ref = take(2)
    images = groups * members
    own, member = places(members)
    width = heads * HEAD_DIM
    length = image_refs[0].shape[0]
    ahead = 2 * member - 1

    for ref, (step, flip) in zip(image_refs, slots):
        if step is None:
            pictures[flip // members, (flip % members) * length : (flip % members + 1) * length, :] = ref[...]
            continue
        place = own + step * ahead
        who = jnp.bitwise_xor(member, flip)

        @pl.when((place >= 0) & (place < groups))
        def _(ref=ref, place=place, who=who):
            pictures[place, pl.ds(pl.multiple_of(who * length, 16), length), :] = ref[...]

    if first:
        pair_ref[...] = jnp.zeros_like(pair_ref)
        single_ref[...] = jnp.zeros_like(single_ref)
    else:
        for new, old in zip((key_ref, value_ref, query_ref, pair_ref, single_ref), state_in):
            new[...] = old[...]

    count = jnp.int32(0)
    for place in range(groups):
        for target in range(images):
            away = jnp.maximum(jnp.abs(place - own), jnp.abs(target // members - own))
            amount = table_ref[place * members + member, target]
            list_ref[count] = place * images + target
            count = count + ((amount > 0) & (away > low) & (away <= high)).astype(jnp.int32)

    def project(place, carry):
        away = jnp.abs(place - own)

        @pl.when((away > low) & (away <= high))
        def _():
            both = jnp.dot(pictures[place], weights[:, : 2 * width], preferred_element_type=F32).astype(BF16)
            aligned = width // 128 * 128
            for who in range(members):
                rows = both[who * length : (who + 1) * length]
                key_ref[place * members + who] = rows[:, :width]
                value_ref[place * members + who] = rows[:, aligned:].T[width - aligned :]
            rows = pictures[place, pl.ds(pl.multiple_of(member * length, 16), length), :]
            query = jnp.dot(rows, weights[:, 2 * width : 3 * width], preferred_element_type=F32).astype(BF16)
            flipped = query.T
            head = lax.broadcasted_iota(jnp.int32, flipped.shape, 0) // HEAD_DIM
            for h in range(heads):
                query_ref[place, :, h * length : (h + 1) * length] = jnp.where(
                    head == h, flipped, jnp.zeros_like(flipped)
                )

        return carry

    lax.fori_loop(0, groups, project, 0)

    scale = math.log2(math.e) / math.sqrt(HEAD_DIM)
    paired = heads // 2

    def block(number, carry):
        entries = []
        for u in range(TOGETHER):
            at = number * TOGETHER + u
            there = at < count
            entry = list_ref[jnp.where(there, at, 0)]
            place, target = entry // images, entry % images
            amount = jnp.where(there, table_ref[place * members + member, target], 0.0)
            entries.append((place, target, amount))
        scores = [jnp.dot(key_ref[t], query_ref[s], preferred_element_type=F32) for s, t, _ in entries]
        expos, factors = [], []
        for each, (_, _, amount) in zip(scores, entries):
            largest = jnp.max(each, axis=0, keepdims=True)
            expo = jnp.exp2((each - largest) * scale)
            total = jnp.sum(expo, axis=0, keepdims=True)
            expos.append(expo.astype(BF16))
            factors.append(amount / total)
        parts = []
        for (_, target, _), expo, factor in zip(entries, expos, factors):
            for j in range(paired):
                rows, lanes = slice(2 * j * HEAD_DIM, 2 * (j + 1) * HEAD_DIM), slice(2 * j * length, 2 * (j + 1) * length)
                part = jnp.dot(value_ref[target, rows, :], expo[:, lanes], preferred_element_type=F32)
                parts.append(part * factor[:, lanes])
            if heads % 2:
                rows, lanes = slice((heads - 1) * HEAD_DIM, None), slice((heads - 1) * length, None)
                part = jnp.dot(value_ref[target, rows, :], expo[:, lanes], preferred_element_type=F32)
                parts.append(part * factor[:, lanes])
        for place, _, _ in entries:
            for j in range(paired):
                pair_ref[place, j] += parts.pop(0)
            if heads % 2:
                single_ref[place] += parts.pop(0)
        return carry

    lax.fori_loop(0, (count + TOGETHER - 1) // TOGETHER, block, 0)

    if last:
        for k in range(groups):
            place = jnp.bitwise_xor(own, k)
            total = jnp.float32(1.0)
            for target in range(images):
                total += table_ref[place * members + member, target]
            pieces = []
            for h in range(heads):
                if h == heads - 1 and heads % 2:
                    pieces.append(single_ref[place])
                else:
                    at = h % 2
                    pieces.append(
                        pair_ref[place, h // 2, at * HEAD_DIM : (at + 1) * HEAD_DIM, at * length : (at + 1) * length]
                    )
            whole = (jnp.concatenate(pieces, axis=0) / total).astype(BF16).T
            half = length // 2
            out_refs[k][:, :width] = whole[:half]
            out_refs[k][:, width:] = whole[half:]


def output_kernel(cfg, *refs):
    groups, members = cfg
    weights = refs[0]
    part_refs = refs[1 : 1 + groups]
    out_ref, gathered = refs[1 + groups :]
    own, _ = places(members)
    half = part_refs[0].shape[0]
    width = part_refs[0].shape[1] // 2
    for k in range(groups):
        source = jnp.bitwise_xor(own, k)
        gathered[source, :half] = part_refs[k][:, :width]
        gathered[source, half:] = part_refs[k][:, width:]
    whole = jnp.concatenate([gathered[h] for h in range(groups)], axis=1)
    out_ref[...] = jnp.dot(whole, weights[...], preferred_element_type=F32).astype(BF16)


def shards(mesh_shape, *arrays):
    return device_step(mesh_shape, *arrays)


def device_step(mesh_shape, tokens, norm_gain, w_query, w_key, w_value, w_out, owner_map, pair_images, pair_count, confidence):
    devices, sharers = mesh_shape["shard"], mesh_shape["group"]
    groups = math.gcd(HEADS & -HEADS, devices)
    members = devices // groups
    heads = HEADS // groups
    width = heads * HEAD_DIM
    length, features = tokens.shape[1:]
    rows = w_query.shape[0]
    small = (owner_map, pair_images.T, pair_count, confidence.T)
    lanes = round_up(3 * width + devices, 128)
    relayed = members == 2 and sharers & (sharers - 1) == 0
    relayed = relayed and rows % (8 * sharers) == 0 and rows % 16 == 0 and rows // sharers >= devices
    relayed = relayed and devices % 8 == 0 and (groups - 1) * rows % 16 == 0
    across = lambda k: [(i, i ^ (k * members)) for i in range(devices)]
    exchange = lambda x, k: lax.ppermute(x, "shard", across(k))

    stage_images, stage_slots = [], []
    if relayed:
        part = rows // sharers
        swap = lambda x: lax.ppermute(x, "shard", [(i, i ^ 1) for i in range(devices)])
        share = lambda x, j: lax.ppermute(
            x,
            ("group", "shard"),
            [(g * devices + i, (g ^ j) * devices + i) for g in range(sharers) for i in range(devices)],
        )
        arrays = (w_query, w_key, w_value, w_out, tokens[0], norm_gain)
        normed, own_block, *messages = call(
            functools.partial(message_kernel, (groups, members, sharers)),
            [struct((length, features)), struct((rows, lanes))] + [struct((part, lanes + features))] * (groups - 1),
            (),
            (),
            [pltpu.SMEM(x.shape, x.dtype) for x in small]
            + [pltpu.VMEM(x.shape, x.dtype) for x in arrays]
            + [pltpu.VMEM((4, rows, features), F32), pltpu.SemaphoreType.DMA((10,))],
            megabytes=62,
            whole=(*small, *arrays),
        )
        messages = [exchange(messages[k - 1], k) for k in range(1, groups)]
        own_a, own_b = normed, swap(normed)
        images, slots = [own_a, own_b], [(0, 0), (0, 1)]
        a, b = own_a, own_b
        for k in range(1, groups):
            pairs = [(2 * z, 2 * z + 2) for z in range(k - 1, groups - 1)]
            pairs += [(2 * z + 1, 2 * z - 1) for z in range(1, groups - k + 1)]
            a, b = lax.ppermute(a, "shard", pairs), lax.ppermute(b, "shard", pairs)
            images += [a, b, swap(a), swap(b)]
            slots += [(k, 0), (k, 1), (-k, 1), (-k, 0)]
            if k == 1 or k == groups - 1:
                stage_images.append(images)
                stage_slots.append(tuple(slots))
                images, slots = [], []

        packed = call(packed_kernel, struct(((groups - 1) * part, lanes + features)), (), messages)
        shared = [packed] + [share(packed, j) for j in range(1, sharers)]
        mine, out_mine = call(
            functools.partial(gathered_kernel, (groups, rows, sharers, devices, 3 * width)),
            [struct((groups * rows, lanes)), struct((groups * rows, features))],
            (),
            (own_block, w_out, *shared),
            [pltpu.VMEM(((groups - 1) * rows, lanes + features), F32)],
        )
        other, out_other = swap(mine), swap(out_mine)
        join = functools.partial(joined_kernel, (groups, members, rows))
        weights = call(join, struct((features, lanes)), (), (mine, other))
        table = sum(
            x[k * rows : k * rows + devices, 3 * width : 3 * width + devices].astype(F32)
            for x in (mine, other)
            for k in range(groups)
        )
        out_weights = lambda: call(join, struct((features, features)), (), (out_mine, out_other))
    else:
        gather = lambda x: lax.all_gather(x, "shard", axis=0, tiled=True)
        own = lax.axis_index("shard") // members
        columns = lambda w: lax.dynamic_slice_in_dim(gather(w), own * width, width, 1)
        weights = jnp.concatenate([columns(w) for w in (w_key, w_value, w_query)], axis=1)
        table = call(table_kernel, struct((round_up(devices, 16), 128)), small, ())
        table = jnp.sum(gather(table[None])[:, :devices, :devices].astype(F32), axis=0)
        normed = call(norm_kernel, struct((length, features)), (), (tokens[0], norm_gain))
        every = gather(normed[None])
        stage_images.append([every[i] for i in range(devices)])
        stage_slots.append(tuple((None, i) for i in range(devices)))
        out_weights = lambda: gather(w_out)

    state_shapes = (
        struct((devices, length, width)),
        struct((devices, width, length)),
        struct((groups, width, heads * length)),
        struct((groups, max(heads // 2, 1), 2 * HEAD_DIM, 2 * length), F32),
        struct((groups, HEAD_DIM, length), F32),
    )
    part_shapes = tuple(struct((length // 2, 2 * width)) for _ in range(groups))
    state = ()
    stages = len(stage_images)
    bounds = [-1] + [1 if s < stages - 1 else groups for s in range(stages)]
    for s in range(stages):
        last = s == stages - 1
        cfg = (groups, members, heads, bounds[s], bounds[s + 1], stage_slots[s], last)
        scratch = [pltpu.VMEM((groups, members * length, features), BF16), pltpu.SMEM((groups * devices + 1,), jnp.int32)]
        if last:
            scratch = [pltpu.VMEM(x.shape, x.dtype) for x in state_shapes] + scratch
        state = call(
            functools.partial(attention_kernel, cfg),
            part_shapes if last else state_shapes,
            (table,),
            (weights, *stage_images[s], *state),
            scratch,
            megabytes=24 if relayed else 60,
        )

    parts = [state[0]] + [exchange(state[k], k) for k in range(1, groups)]
    out = call(
        functools.partial(output_kernel, (groups, members)),
        struct((length, features)),
        (),
        (out_weights(), *parts),
        [pltpu.VMEM((groups, length, width), BF16)],
    )
    return out[None]


def solution(mesh):
    in_specs = (
        P(("group", "shard"), None, None),
        P(),
        P("shard", None),
        P("shard", None),
        P("shard", None),
        P("shard", None),
        P("group", None),
        P(("group", "shard"), None),
        P(("group", "shard")),
        P(("group", "shard"), None),
    )
    out_specs = P(("group", "shard"), None, None)
    return jax.shard_map(
        functools.partial(shards, dict(mesh.shape)),
        mesh=mesh,
        in_specs=in_specs,
        out_specs=out_specs,
        check_vma=False,
    )
```

```python
import functools
import math

import jax
import jax.numpy as jnp
from jax import lax
from jax.experimental import pallas as pl
from jax.experimental.pallas import tpu as pltpu
from jax.sharding import PartitionSpec as P


HEADS = 12
HEAD_DIM = 64
ONES = 16
TOGETHER = 4

F32 = jnp.float32
BF16 = jnp.bfloat16
HBM_SPEC = pl.BlockSpec(memory_space=pltpu.HBM)
SMEM_SPEC = pl.BlockSpec(memory_space=pltpu.SMEM)
VMEM_SPEC = pl.BlockSpec(memory_space=pltpu.VMEM)


def round_up(value, multiple):
    return -(-value // multiple) * multiple


def struct(shape, dtype=BF16):
    return jax.ShapeDtypeStruct(shape, dtype)


def call(kernel, out_shape, smem, vmem, scratch=(), megabytes=16, whole=()):
    many = isinstance(out_shape, (tuple, list))
    return pl.pallas_call(
        kernel,
        out_shape=tuple(out_shape) if many else out_shape,
        in_specs=[SMEM_SPEC] * len(smem) + [VMEM_SPEC] * len(vmem) + [HBM_SPEC] * len(whole),
        out_specs=(VMEM_SPEC,) * len(out_shape) if many else VMEM_SPEC,
        scratch_shapes=list(scratch),
        compiler_params=pltpu.CompilerParams(vmem_limit_bytes=megabytes * 1024 * 1024),
    )(*smem, *vmem, *whole)


def places(members):
    position = lax.axis_index("shard")
    return position // members, position % members


def direction_table(owner_ref, pairs_ref, count_ref, conf_ref, shape):
    row = lax.broadcasted_iota(jnp.int32, shape, 0)
    column = lax.broadcasted_iota(jnp.int32, shape, 1)
    table = jnp.zeros(shape, jnp.int32)
    for p in range(pairs_ref.shape[1]):
        first = owner_ref[0, pairs_ref[0, p]]
        second = owner_ref[0, pairs_ref[1, p]]
        listed = p < count_ref[0]
        forward = jnp.where(listed, conf_ref[0, p], 0)
        backward = jnp.where(listed, conf_ref[1, p], 0)
        table += jnp.where((row == first) & (column == second), forward, 0)
        table += jnp.where((row == second) & (column == first), backward, 0)
    return table.astype(F32)


def table_kernel(owner_ref, pairs_ref, count_ref, conf_ref, table_ref):
    table_ref[...] = direction_table(owner_ref, pairs_ref, count_ref, conf_ref, table_ref.shape).astype(BF16)


def message_kernel(cfg, *refs):
    groups, members, sharers = cfg
    sources, refs = refs[:10], refs[10:]
    normed_ref, own_ref, message_refs, refs = refs[0], refs[1], refs[2 : 1 + groups], refs[1 + groups :]
    copied, wide, sem = refs[:10], refs[10], refs[11]
    owner_ref, pairs_ref, count_ref, conf_ref, query_ref, key_ref, value_ref, out_ref, tokens_ref, gain_ref = copied
    copies = [pltpu.make_async_copy(source, into, sem.at[i]) for i, (source, into) in enumerate(zip(sources, copied))]
    for each in copies:
        each.start()
    own, _ = places(members)
    rows, features = query_ref.shape
    width = features // groups
    part = rows // sharers
    start = pl.multiple_of(lax.axis_index("group") * part, 8)
    lanes = own_ref.shape[1]
    for each in copies:
        each.wait()
    for i, ref in enumerate((key_ref, value_ref, query_ref, out_ref)):
        wide[i] = ref[...].astype(F32)
    for h in range(groups):
        cut = slice(h * width, (h + 1) * width)

        @pl.when(own == h)
        def _(cut=cut):
            for i, ref in enumerate((key_ref, value_ref, query_ref)):
                own_ref[:, i * width : (i + 1) * width] = ref[:, cut]

        for k in range(1, groups):

            @pl.when(own == h ^ k)
            def _(k=k, cut=cut):
                for i in range(3):
                    message_refs[k - 1][:, i * width : (i + 1) * width] = wide[i, pl.ds(start, part), cut].astype(BF16)

    images = groups * members
    table = direction_table(owner_ref, pairs_ref, count_ref, conf_ref, (images, lanes - 3 * width)).astype(BF16)
    own_ref[:images, 3 * width :] = table
    for ref in message_refs:
        ref[:, lanes:] = wide[3, pl.ds(start, part), :].astype(BF16)
        ref[:images, 3 * width : lanes] = table
    normed_ref[...] = layer_norm(tokens_ref[...], gain_ref[...])


def layer_norm(tokens, gain):
    values = tokens.astype(F32)
    average = jnp.mean(values, axis=-1, keepdims=True)
    centred = values - average
    variance = jnp.mean(centred * centred, axis=-1, keepdims=True)
    return (centred * lax.rsqrt(variance + 1e-05) * gain.reshape(1, gain.shape[0])).astype(BF16)


def norm_kernel(tokens_ref, gain_ref, normed_ref):
    normed_ref[...] = layer_norm(tokens_ref[...], gain_ref[...])


def packed_kernel(*refs):
    message_refs, packed_ref = refs[:-1], refs[-1]
    part = message_refs[0].shape[0]
    for k, ref in enumerate(message_refs):
        packed_ref[k * part : (k + 1) * part] = ref[...]


def gathered_kernel(cfg, own_ref, out_ref, *refs):
    groups, rows, sharers, images, spare = cfg
    shared_refs = refs[:sharers]
    in_block, out_block, wide = refs[sharers:]
    part = rows // sharers
    lanes = in_block.shape[1]
    mine = lax.axis_index("group")
    in_block[:rows] = own_ref[...]
    out_block[:rows] = out_ref[...]
    for j in range(sharers):
        for k in range(1, groups):
            start = pl.multiple_of((k - 1) * rows + jnp.bitwise_xor(mine, j) * part, 8)
            wide[pl.ds(start, part), :] = shared_refs[j][(k - 1) * part : k * part, :].astype(F32)
    in_block[rows:] = wide[:, :lanes].astype(BF16)
    out_block[rows:] = wide[:, lanes:].astype(BF16)
    for k in range(1, groups):
        in_block[k * rows : k * rows + images, spare:] = shared_refs[0][(k - 1) * part : (k - 1) * part + images, spare:lanes]


def joined_kernel(cfg, mine_ref, other_ref, whole_ref):
    groups, members, rows = cfg
    own, member = places(members)
    for k in range(groups):
        source = jnp.bitwise_xor(own, k) * members
        for ref, who in ((mine_ref, member), (other_ref, 1 - member)):
            start = pl.multiple_of((source + who) * rows, 16)
            whole_ref[pl.ds(start, rows), :] = ref[k * rows : (k + 1) * rows, :]


def attention_kernel(cfg, *refs):
    groups, members, heads, reach, fresh, slots, near, sent, _ = cfg
    low, high = reach
    refs = list(refs)
    take = lambda count: [refs.pop(0) for _ in range(count)]
    table_ref, weights = take(2)
    image_refs = take(len(slots))
    first = low < 0
    state_in = [] if first else take(5)
    out_refs = take(len(sent))
    if fresh:
        key_ref, value_ref, query_ref = take(3)
    else:
        key_ref, value_ref, query_ref = state_in[:3]
    pair_ref, single_ref = take(2)
    pictures, list_ref = take(2)
    images = groups * members
    own, member = places(members)
    width = heads * HEAD_DIM
    length = value_ref.shape[2]
    paired = heads // 2
    paired_rows = 2 * paired * HEAD_DIM
    ahead = 2 * member - 1

    for ref, (step, flip) in zip(image_refs, slots):
        if step is None:
            pictures[flip // members, (flip % members) * length : (flip % members + 1) * length, :] = ref[...]
            continue
        place = own + step * ahead
        who = jnp.bitwise_xor(member, flip)

        @pl.when((place >= 0) & (place < groups))
        def _(ref=ref, place=place, who=who):
            pictures[place, pl.ds(pl.multiple_of(who * length, 16), length), :] = ref[...]

    if first:
        pair_ref[...] = jnp.zeros_like(pair_ref)
        single_ref[...] = jnp.zeros_like(single_ref)
        value_ref[:, paired_rows : paired_rows + ONES, :] = jnp.ones((images, ONES, length), BF16)
    else:
        new = (key_ref, value_ref, query_ref, pair_ref, single_ref)
        for into, old in list(zip(new, state_in))[0 if fresh else 3 :]:
            into[...] = old[...]

    count = jnp.int32(0)
    for place in range(groups):
        apart = jnp.bitwise_xor(own, place)
        for target in range(images):
            away = jnp.maximum(jnp.abs(place - own), jnp.abs(target // members - own))
            amount = table_ref[place * members + member, target]
            list_ref[count] = place * images + target
            chosen = (amount > 0) & (away > low) & (away <= high) & (apart >= near[0]) & (apart < near[1])
            count = count + chosen.astype(jnp.int32)

    def project(place, carry):
        away = jnp.abs(place - own)

        @pl.when((away > low) & (away <= high))
        def _():
            rows_in = pictures[place, pl.ds(pl.multiple_of(member * length, 16), length), :]
            both = jnp.dot(pictures[place], weights[:, : 2 * width], preferred_element_type=F32).astype(BF16)
            query = jnp.dot(rows_in, weights[:, 2 * width : 3 * width], preferred_element_type=F32).astype(BF16)
            aligned = width // 128 * 128
            for who in range(members):
                image = place * members + who
                rows = both[who * length : (who + 1) * length]
                key_ref[image] = rows[:, :width]
                flipped = rows[:, aligned:].T[width - aligned :]
                value_ref[image, :paired_rows] = flipped[:paired_rows]
                if heads % 2:
                    value_ref[image, paired_rows + ONES :] = flipped[paired_rows:]
            flipped = query.T
            head = lax.broadcasted_iota(jnp.int32, flipped.shape, 0) // HEAD_DIM
            for h in range(heads):
                query_ref[place, :, h * length : (h + 1) * length] = jnp.where(
                    head == h, flipped, jnp.zeros_like(flipped)
                )

        return carry

    if fresh:
        lax.fori_loop(0, groups, project, 0)

    scale = math.log2(math.e) / math.sqrt(HEAD_DIM)

    def block(number, carry):
        entries = []
        for u in range(TOGETHER):
            at = number * TOGETHER + u
            there = at < count
            entry = list_ref[jnp.where(there, at, 0)]
            place, target = entry // images, entry % images
            amount = jnp.where(there, table_ref[place * members + member, target], 0.0)
            entries.append((place, target, amount))
        scores = [jnp.dot(key_ref[t], query_ref[s], preferred_element_type=F32) for s, t, _ in entries]
        expos = []
        for each in scores:
            largest = jnp.max(each, axis=0, keepdims=True)
            expos.append(jnp.exp2((each - largest) * scale).astype(BF16))
        parts = []
        for (_, target, amount), expo in zip(entries, expos):
            values = value_ref[target]
            for j in range(paired):
                lanes = slice(2 * j * length, 2 * (j + 1) * length)
                rows = values[2 * j * HEAD_DIM : 2 * (j + 1) * HEAD_DIM]
                if j == paired - 1:
                    rows = values[2 * j * HEAD_DIM : paired_rows + ONES]
                else:
                    rows = jnp.concatenate([rows, values[paired_rows : paired_rows + ONES]], axis=0)
                part = jnp.dot(rows, expo[:, lanes], preferred_element_type=F32)
                parts.append(part[: 2 * HEAD_DIM] * (amount / part[2 * HEAD_DIM : 2 * HEAD_DIM + 1]))
            if heads % 2:
                part = jnp.dot(values[paired_rows:], expo[:, (heads - 1) * length :], preferred_element_type=F32)
                parts.append(part[ONES:] * (amount / part[:1]))
        for place, _, _ in entries:
            for j in range(paired):
                pair_ref[place, j] += parts.pop(0)
            if heads % 2:
                single_ref[place] += parts.pop(0)
        return carry

    lax.fori_loop(0, (count + TOGETHER - 1) // TOGETHER, block, 0)

    for k, out_ref in zip(sent, out_refs):
        place = jnp.bitwise_xor(own, k)
        total = jnp.float32(1.0)
        for target in range(images):
            total += table_ref[place * members + member, target]
        pieces = []
        for h in range(heads):
            if h == heads - 1 and heads % 2:
                pieces.append(single_ref[place])
            else:
                at = h % 2
                pieces.append(
                    pair_ref[place, h // 2, at * HEAD_DIM : (at + 1) * HEAD_DIM, at * length : (at + 1) * length]
                )
        whole = (jnp.concatenate(pieces, axis=0) / total).astype(BF16).T
        half = length // 2
        out_ref[:, :width] = whole[:half]
        out_ref[:, width:] = whole[half:]


def output_kernel(cfg, *refs):
    groups, members = cfg
    weights = refs[0]
    part_refs = refs[1 : 1 + groups]
    out_ref, gathered = refs[1 + groups :]
    own, _ = places(members)
    half = part_refs[0].shape[0]
    width = part_refs[0].shape[1] // 2
    for k in range(groups):
        source = jnp.bitwise_xor(own, k)
        gathered[source, :half] = part_refs[k][:, :width]
        gathered[source, half:] = part_refs[k][:, width:]
    whole = jnp.concatenate([gathered[h] for h in range(groups)], axis=1)
    out_ref[...] = jnp.dot(whole, weights[...], preferred_element_type=F32).astype(BF16)


def shards(mesh_shape, *arrays):
    return device_step(mesh_shape, *arrays)


def device_step(mesh_shape, tokens, norm_gain, w_query, w_key, w_value, w_out, owner_map, pair_images, pair_count, confidence):
    devices, sharers = mesh_shape["shard"], mesh_shape["group"]
    groups = math.gcd(HEADS & -HEADS, devices)
    members = devices // groups
    heads = HEADS // groups
    width = heads * HEAD_DIM
    length, features = tokens.shape[1:]
    rows = w_query.shape[0]
    small = (owner_map, pair_images.T, pair_count, confidence.T)
    lanes = round_up(3 * width + devices, 128)
    relayed = members == 2 and sharers & (sharers - 1) == 0
    relayed = relayed and rows % (8 * sharers) == 0 and rows % 16 == 0 and rows // sharers >= devices
    relayed = relayed and devices % 8 == 0 and (groups - 1) * rows % 16 == 0
    across = lambda k: [(i, i ^ (k * members)) for i in range(devices)]
    exchange = lambda x, k: lax.ppermute(x, "shard", across(k))

    stage_images, stage_slots = [], []
    if relayed:
        part = rows // sharers
        swap = lambda x: lax.ppermute(x, "shard", [(i, i ^ 1) for i in range(devices)])
        share = lambda x, j: lax.ppermute(
            x,
            ("group", "shard"),
            [(g * devices + i, (g ^ j) * devices + i) for g in range(sharers) for i in range(devices)],
        )
        arrays = (w_query, w_key, w_value, w_out, tokens[0], norm_gain)
        normed, own_block, *messages = call(
            functools.partial(message_kernel, (groups, members, sharers)),
            [struct((length, features)), struct((rows, lanes))] + [struct((part, lanes + features))] * (groups - 1),
            (),
            (),
            [pltpu.SMEM(x.shape, x.dtype) for x in small]
            + [pltpu.VMEM(x.shape, x.dtype) for x in arrays]
            + [pltpu.VMEM((4, rows, features), F32), pltpu.SemaphoreType.DMA((10,))],
            megabytes=62,
            whole=(*small, *arrays),
        )
        messages = [exchange(messages[k - 1], k) for k in range(1, groups)]
        own_a, own_b = normed, swap(normed)
        images, slots = [own_a, own_b], [(0, 0), (0, 1)]
        a, b = own_a, own_b
        for k in range(1, groups):
            pairs = [(2 * z, 2 * z + 2) for z in range(k - 1, groups - 1)]
            pairs += [(2 * z + 1, 2 * z - 1) for z in range(1, groups - k + 1)]
            a, b = lax.ppermute(a, "shard", pairs), lax.ppermute(b, "shard", pairs)
            images += [a, b, swap(a), swap(b)]
            slots += [(k, 0), (k, 1), (-k, 1), (-k, 0)]
            if k == 1 or k == groups - 1:
                stage_images.append(images)
                stage_slots.append(tuple(slots))
                images, slots = [], []

        packed = call(packed_kernel, struct(((groups - 1) * part, lanes + features)), (), messages)
        shared = [packed] + [share(packed, j) for j in range(1, sharers)]
        mine, out_mine = call(
            functools.partial(gathered_kernel, (groups, rows, sharers, devices, 3 * width)),
            [struct((groups * rows, lanes)), struct((groups * rows, features))],
            (),
            (own_block, w_out, *shared),
            [pltpu.VMEM(((groups - 1) * rows, lanes + features), F32)],
        )
        other, out_other = swap(mine), swap(out_mine)
        join = functools.partial(joined_kernel, (groups, members, rows))
        weights = call(join, struct((features, lanes)), (), (mine, other))
        table = sum(
            x[k * rows : k * rows + devices, 3 * width : 3 * width + devices].astype(F32)
            for x in (mine, other)
            for k in range(groups)
        )
        out_weights = lambda: call(join, struct((features, features)), (), (out_mine, out_other))
    else:
        gather = lambda x: lax.all_gather(x, "shard", axis=0, tiled=True)
        own = lax.axis_index("shard") // members
        columns = lambda w: lax.dynamic_slice_in_dim(gather(w), own * width, width, 1)
        weights = jnp.concatenate([columns(w) for w in (w_key, w_value, w_query)], axis=1)
        table = call(table_kernel, struct((round_up(devices, 16), 128)), small, ())
        table = jnp.sum(gather(table[None])[:, :devices, :devices].astype(F32), axis=0)
        normed = call(norm_kernel, struct((length, features)), (), (tokens[0], norm_gain))
        normed = gather(normed[None])
        stage_images.append([normed[i] for i in range(devices)])
        stage_slots.append(tuple((None, i) for i in range(devices)))
        out_weights = lambda: gather(w_out)

    state_shapes = (
        struct((devices, length, width)),
        struct((devices, width + ONES, length)),
        struct((groups, width, heads * length)),
        struct((groups, max(heads // 2, 1), 2 * HEAD_DIM, 2 * length), F32),
        struct((groups, HEAD_DIM, length), F32),
    )
    part_shape = struct((length // 2, 2 * width))
    every = tuple(range(groups))
    far, near = every[: groups // 2 - 1 : -1], every[: groups // 2]
    if relayed:
        stages = (
            ((-1, 1), True, (0, groups), (), True),
            ((1, groups), True, (0, groups), far + near, False),
        )
    else:
        stages = (((-1, groups), True, (0, groups), every, False),)
    parts, state = {}, ()
    for s, (reach, fresh, asked, sent, keep) in enumerate(stages):
        cfg = (groups, members, heads, reach, fresh, stage_slots[s], asked, sent, keep)
        scratch = [pltpu.VMEM((groups, members * length, features), BF16), pltpu.SMEM((groups * devices + 1,), jnp.int32)]
        shapes = [part_shape] * len(sent)
        if keep:
            shapes += state_shapes
        else:
            scratch = [pltpu.VMEM(x.shape, x.dtype) for x in state_shapes[0 if fresh else 3 :]] + scratch
        results = call(
            functools.partial(attention_kernel, cfg),
            shapes,
            (table,),
            (weights, *stage_images[s], *state),
            scratch,
            megabytes=24 if relayed else 60,
        )
        for k, part in zip(sent, results):
            parts[k] = exchange(part, k) if k else part
        state = results[len(sent) :]
    parts = [parts[k] for k in every]
    out = call(
        functools.partial(output_kernel, (groups, members)),
        struct((length, features)),
        (),
        (out_weights(), *parts),
        [pltpu.VMEM((groups, length, width), BF16)],
    )
    return out[None]


def solution(mesh):
    in_specs = (
        P(("group", "shard"), None, None),
        P(),
        P("shard", None),
        P("shard", None),
        P("shard", None),
        P("shard", None),
        P("group", None),
        P(("group", "shard"), None),
        P(("group", "shard")),
        P(("group", "shard"), None),
    )
    out_specs = P(("group", "shard"), None, None)
    return jax.shard_map(
        functools.partial(shards, dict(mesh.shape)),
        mesh=mesh,
        in_specs=in_specs,
        out_specs=out_specs,
        check_vma=False,
    )
```

```python
import functools
import math

import jax
import jax.numpy as jnp
from jax import lax
from jax.experimental import pallas as pl
from jax.experimental.pallas import tpu as pltpu
from jax.sharding import PartitionSpec as P


HEADS = 12
HEAD_DIM = 64
ONES = 16
TOGETHER = 4

F32 = jnp.float32
BF16 = jnp.bfloat16
HBM_SPEC = pl.BlockSpec(memory_space=pltpu.HBM)
SMEM_SPEC = pl.BlockSpec(memory_space=pltpu.SMEM)
VMEM_SPEC = pl.BlockSpec(memory_space=pltpu.VMEM)


def round_up(value, multiple):
    return -(-value // multiple) * multiple


def struct(shape, dtype=BF16):
    return jax.ShapeDtypeStruct(shape, dtype)


def call(kernel, out_shape, smem, vmem, scratch=(), megabytes=16, whole=(), out_spec=VMEM_SPEC):
    many = isinstance(out_shape, (tuple, list))
    return pl.pallas_call(
        kernel,
        out_shape=tuple(out_shape) if many else out_shape,
        in_specs=[SMEM_SPEC] * len(smem) + [VMEM_SPEC] * len(vmem) + [HBM_SPEC] * len(whole),
        out_specs=(out_spec,) * len(out_shape) if many else out_spec,
        scratch_shapes=list(scratch),
        compiler_params=pltpu.CompilerParams(vmem_limit_bytes=megabytes * 1024 * 1024),
    )(*smem, *vmem, *whole)


def places(members):
    position = lax.axis_index("shard")
    return position // members, position % members


def direction_table(owner_ref, pairs_ref, count_ref, conf_ref, shape):
    row = lax.broadcasted_iota(jnp.int32, shape, 0)
    column = lax.broadcasted_iota(jnp.int32, shape, 1)
    table = jnp.zeros(shape, jnp.int32)
    for p in range(pairs_ref.shape[1]):
        first = owner_ref[0, pairs_ref[0, p]]
        second = owner_ref[0, pairs_ref[1, p]]
        listed = p < count_ref[0]
        forward = jnp.where(listed, conf_ref[0, p], 0)
        backward = jnp.where(listed, conf_ref[1, p], 0)
        table += jnp.where((row == first) & (column == second), forward, 0)
        table += jnp.where((row == second) & (column == first), backward, 0)
    return table.astype(F32)


def table_kernel(owner_ref, pairs_ref, count_ref, conf_ref, table_ref):
    table_ref[...] = direction_table(owner_ref, pairs_ref, count_ref, conf_ref, table_ref.shape).astype(BF16)


def message_kernel(cfg, *refs):
    groups, members, sharers = cfg
    sources, refs = refs[:10], refs[10:]
    results, refs = refs[: 1 + groups], refs[1 + groups :]
    small, whole, parts, made, (in_sem, out_sem) = refs[:4], refs[4:9], refs[9:13], refs[13:-2], refs[-2:]
    owner_ref, pairs_ref, count_ref, conf_ref = small
    tokens_ref, gain_ref = whole[3:]
    normed_ref, own_ref, message_refs = made[0], made[1], made[2:]
    own, _ = places(members)
    rows, features = whole[0].shape
    width = features // groups
    part = rows // sharers
    start = pl.multiple_of(lax.axis_index("group") * part, 8)
    key, value, query, out = (sources[i] for i in (5, 6, 4, 7))
    moves = [(source, into) for source, into in zip(sources[:4], small)]
    moves += [(source.at[pl.ds(start, part), :], into) for source, into in zip((key, value, query, out), parts)]
    moves += [(source, into) for source, into in zip((key, value, query, sources[8], sources[9]), whole)]
    moves = [pltpu.make_async_copy(source, into, in_sem.at[i]) for i, (source, into) in enumerate(moves)]
    stores = [pltpu.make_async_copy(source, into, out_sem.at[i]) for i, (source, into) in enumerate(zip(made, results))]
    for move in moves:
        move.start()

    lanes = own_ref.shape[1]
    for move in moves[:8]:
        move.wait()
    images = groups * members
    table = direction_table(owner_ref, pairs_ref, count_ref, conf_ref, (images, lanes - 3 * width)).astype(BF16)
    for h in range(groups):
        for k in range(1, groups):

            @pl.when(own == h ^ k)
            def _(k=k, cut=slice(h * width, (h + 1) * width)):
                for i in range(3):
                    message_refs[k - 1][:, i * width : (i + 1) * width] = parts[i][:, cut]

    for ref in message_refs:
        ref[:, lanes:] = parts[3][...]
        ref[:images, 3 * width : lanes] = table
    for store in stores[2:]:
        store.start()
    for move in moves[8:]:
        move.wait()
    normed_ref[...] = layer_norm(tokens_ref[...], gain_ref[...])
    stores[0].start()
    for h in range(groups):

        @pl.when(own == h)
        def _(cut=slice(h * width, (h + 1) * width)):
            for i, ref in enumerate(whole[:3]):
                own_ref[:, i * width : (i + 1) * width] = ref[:, cut]

    own_ref[:images, 3 * width :] = table
    stores[1].start()
    for store in stores:
        store.wait()


def layer_norm(tokens, gain):
    values = tokens.astype(F32)
    average = jnp.mean(values, axis=-1, keepdims=True)
    centred = values - average
    variance = jnp.mean(centred * centred, axis=-1, keepdims=True)
    return (centred * lax.rsqrt(variance + 1e-05) * gain.reshape(1, gain.shape[0])).astype(BF16)


def norm_kernel(tokens_ref, gain_ref, normed_ref):
    normed_ref[...] = layer_norm(tokens_ref[...], gain_ref[...])


def packed_kernel(*refs):
    message_refs, packed_ref = refs[:-1], refs[-1]
    part = message_refs[0].shape[0]
    for k, ref in enumerate(message_refs):
        packed_ref[k * part : (k + 1) * part] = ref[...]


def gathered_kernel(cfg, own_ref, out_ref, *refs):
    groups, rows, sharers, images, spare = cfg
    shared_refs = refs[:sharers]
    in_block, out_block, wide = refs[sharers:]
    part = rows // sharers
    lanes = in_block.shape[1]
    mine = lax.axis_index("group")
    in_block[:rows] = own_ref[...]
    out_block[:rows] = out_ref[...]
    for j in range(sharers):
        for k in range(1, groups):
            start = pl.multiple_of((k - 1) * rows + jnp.bitwise_xor(mine, j) * part, 8)
            wide[pl.ds(start, part), :] = shared_refs[j][(k - 1) * part : k * part, :].astype(F32)
    in_block[rows:] = wide[:, :lanes].astype(BF16)
    out_block[rows:] = wide[:, lanes:].astype(BF16)
    for k in range(1, groups):
        in_block[k * rows : k * rows + images, spare:] = shared_refs[0][(k - 1) * part : (k - 1) * part + images, spare:lanes]


def joined_kernel(cfg, mine_ref, other_ref, whole_ref):
    groups, members, rows = cfg
    own, member = places(members)
    for k in range(groups):
        source = jnp.bitwise_xor(own, k) * members
        for ref, who in ((mine_ref, member), (other_ref, 1 - member)):
            start = pl.multiple_of((source + who) * rows, 16)
            whole_ref[pl.ds(start, rows), :] = ref[k * rows : (k + 1) * rows, :]


def attention_kernel(cfg, *refs):
    groups, members, heads, reach, fresh, slots, near, sent, _ = cfg
    low, high = reach
    refs = list(refs)
    take = lambda count: [refs.pop(0) for _ in range(count)]
    table_ref, weights = take(2)
    image_refs = take(len(slots))
    first = low < 0
    state_in = [] if first else take(5)
    out_refs = take(len(sent))
    if fresh:
        key_ref, value_ref, query_ref = take(3)
    else:
        key_ref, value_ref, query_ref = state_in[:3]
    pair_ref, single_ref = take(2)
    pictures, list_ref = take(2)
    images = groups * members
    own, member = places(members)
    width = heads * HEAD_DIM
    length = value_ref.shape[2]
    paired = heads // 2
    paired_rows = 2 * paired * HEAD_DIM
    ahead = 2 * member - 1

    for ref, (step, flip) in zip(image_refs, slots):
        if step is None:
            pictures[flip // members, (flip % members) * length : (flip % members + 1) * length, :] = ref[...]
            continue
        place = own + step * ahead
        who = jnp.bitwise_xor(member, flip)

        @pl.when((place >= 0) & (place < groups))
        def _(ref=ref, place=place, who=who):
            pictures[place, pl.ds(pl.multiple_of(who * length, 16), length), :] = ref[...]

    if first:
        pair_ref[...] = jnp.zeros_like(pair_ref)
        single_ref[...] = jnp.zeros_like(single_ref)
        value_ref[:, paired_rows : paired_rows + ONES, :] = jnp.ones((images, ONES, length), BF16)
    else:
        new = (key_ref, value_ref, query_ref, pair_ref, single_ref)
        for into, old in list(zip(new, state_in))[0 if fresh else 3 :]:
            into[...] = old[...]

    count = jnp.int32(0)
    for place in range(groups):
        apart = jnp.bitwise_xor(own, place)
        for target in range(images):
            away = jnp.maximum(jnp.abs(place - own), jnp.abs(target // members - own))
            amount = table_ref[place * members + member, target]
            list_ref[count] = place * images + target
            chosen = (amount > 0) & (away > low) & (away <= high) & (apart >= near[0]) & (apart < near[1])
            count = count + chosen.astype(jnp.int32)

    def project(place, carry):
        away = jnp.abs(place - own)

        @pl.when((away > low) & (away <= high))
        def _():
            rows_in = pictures[place, pl.ds(pl.multiple_of(member * length, 16), length), :]
            both = jnp.dot(pictures[place], weights[:, : 2 * width], preferred_element_type=F32).astype(BF16)
            query = jnp.dot(rows_in, weights[:, 2 * width : 3 * width], preferred_element_type=F32).astype(BF16)
            aligned = width // 128 * 128
            for who in range(members):
                image = place * members + who
                rows = both[who * length : (who + 1) * length]
                key_ref[image] = rows[:, :width]
                flipped = rows[:, aligned:].T[width - aligned :]
                value_ref[image, :paired_rows] = flipped[:paired_rows]
                if heads % 2:
                    value_ref[image, paired_rows + ONES :] = flipped[paired_rows:]
            flipped = query.T
            head = lax.broadcasted_iota(jnp.int32, flipped.shape, 0) // HEAD_DIM
            for h in range(heads):
                query_ref[place, :, h * length : (h + 1) * length] = jnp.where(
                    head == h, flipped, jnp.zeros_like(flipped)
                )

        return carry

    if fresh:
        lax.fori_loop(0, groups, project, 0)

    scale = math.log2(math.e) / math.sqrt(HEAD_DIM)

    def block(number, carry):
        entries = []
        for u in range(TOGETHER):
            at = number * TOGETHER + u
            there = at < count
            entry = list_ref[jnp.where(there, at, 0)]
            place, target = entry // images, entry % images
            amount = jnp.where(there, table_ref[place * members + member, target], 0.0)
            entries.append((place, target, amount))
        scores = [jnp.dot(key_ref[t], query_ref[s], preferred_element_type=F32) for s, t, _ in entries]
        expos = []
        for each in scores:
            largest = jnp.max(each, axis=0, keepdims=True)
            expos.append(jnp.exp2((each - largest) * scale).astype(BF16))
        parts = []
        for (_, target, amount), expo in zip(entries, expos):
            values = value_ref[target]
            for j in range(paired):
                lanes = slice(2 * j * length, 2 * (j + 1) * length)
                rows = values[2 * j * HEAD_DIM : 2 * (j + 1) * HEAD_DIM]
                if j == paired - 1:
                    rows = values[2 * j * HEAD_DIM : paired_rows + ONES]
                else:
                    rows = jnp.concatenate([rows, values[paired_rows : paired_rows + ONES]], axis=0)
                part = jnp.dot(rows, expo[:, lanes], preferred_element_type=F32)
                parts.append(part[: 2 * HEAD_DIM] * (amount / part[2 * HEAD_DIM : 2 * HEAD_DIM + 1]))
            if heads % 2:
                part = jnp.dot(values[paired_rows:], expo[:, (heads - 1) * length :], preferred_element_type=F32)
                parts.append(part[ONES:] * (amount / part[:1]))
        for place, _, _ in entries:
            for j in range(paired):
                pair_ref[place, j] += parts.pop(0)
            if heads % 2:
                single_ref[place] += parts.pop(0)
        return carry

    lax.fori_loop(0, (count + TOGETHER - 1) // TOGETHER, block, 0)

    for k, out_ref in zip(sent, out_refs):
        place = jnp.bitwise_xor(own, k)
        total = jnp.float32(1.0)
        for target in range(images):
            total += table_ref[place * members + member, target]
        pieces = []
        for h in range(heads):
            if h == heads - 1 and heads % 2:
                pieces.append(single_ref[place])
            else:
                at = h % 2
                pieces.append(
                    pair_ref[place, h // 2, at * HEAD_DIM : (at + 1) * HEAD_DIM, at * length : (at + 1) * length]
                )
        whole = (jnp.concatenate(pieces, axis=0) / total).astype(BF16).T
        half = length // 2
        out_ref[:, :width] = whole[:half]
        out_ref[:, width:] = whole[half:]


def output_kernel(cfg, *refs):
    groups, members = cfg
    weights = refs[0]
    part_refs = refs[1 : 1 + groups]
    out_ref, gathered = refs[1 + groups :]
    own, _ = places(members)
    half = part_refs[0].shape[0]
    width = part_refs[0].shape[1] // 2
    for k in range(groups):
        source = jnp.bitwise_xor(own, k)
        gathered[source, :half] = part_refs[k][:, :width]
        gathered[source, half:] = part_refs[k][:, width:]
    whole = jnp.concatenate([gathered[h] for h in range(groups)], axis=1)
    out_ref[...] = jnp.dot(whole, weights[...], preferred_element_type=F32).astype(BF16)


def shards(mesh_shape, *arrays):
    return device_step(mesh_shape, *arrays)


def device_step(mesh_shape, tokens, norm_gain, w_query, w_key, w_value, w_out, owner_map, pair_images, pair_count, confidence):
    devices, sharers = mesh_shape["shard"], mesh_shape["group"]
    groups = math.gcd(HEADS & -HEADS, devices)
    members = devices // groups
    heads = HEADS // groups
    width = heads * HEAD_DIM
    length, features = tokens.shape[1:]
    rows = w_query.shape[0]
    small = (owner_map, pair_images.T, pair_count, confidence.T)
    lanes = round_up(3 * width + devices, 128)
    relayed = members == 2 and sharers & (sharers - 1) == 0
    relayed = relayed and rows % (8 * sharers) == 0 and rows % 16 == 0 and rows // sharers >= devices
    relayed = relayed and devices % 8 == 0 and (groups - 1) * rows % 16 == 0
    across = lambda k: [(i, i ^ (k * members)) for i in range(devices)]
    exchange = lambda x, k: lax.ppermute(x, "shard", across(k))

    stage_images, stage_slots = [], []
    if relayed:
        part = rows // sharers
        swap = lambda x: lax.ppermute(x, "shard", [(i, i ^ 1) for i in range(devices)])
        share = lambda x, j: lax.ppermute(
            x,
            ("group", "shard"),
            [(g * devices + i, (g ^ j) * devices + i) for g in range(sharers) for i in range(devices)],
        )
        arrays = (w_query, w_key, w_value, w_out, tokens[0], norm_gain)
        made = [struct((length, features)), struct((rows, lanes))] + [struct((part, lanes + features))] * (groups - 1)
        scratch = [pltpu.SMEM(x.shape, x.dtype) for x in small]
        scratch += [pltpu.VMEM(x.shape, x.dtype) for x in (w_key, w_value, w_query, tokens[0], norm_gain)]
        scratch += [pltpu.VMEM((part, features), BF16)] * 4 + [pltpu.VMEM(x.shape, x.dtype) for x in made]
        scratch += [pltpu.SemaphoreType.DMA((13,)), pltpu.SemaphoreType.DMA((len(made),))]
        normed, own_block, *messages = call(
            functools.partial(message_kernel, (groups, members, sharers)),
            made,
            (),
            (),
            scratch,
            megabytes=62,
            whole=(*small, *arrays),
            out_spec=HBM_SPEC,
        )
        messages = [exchange(messages[k - 1], k) for k in range(1, groups)]
        own_a, own_b = normed, swap(normed)
        images, slots = [own_a, own_b], [(0, 0), (0, 1)]
        a, b = own_a, own_b
        for k in range(1, groups):
            pairs = [(2 * z, 2 * z + 2) for z in range(k - 1, groups - 1)]
            pairs += [(2 * z + 1, 2 * z - 1) for z in range(1, groups - k + 1)]
            a, b = lax.ppermute(a, "shard", pairs), lax.ppermute(b, "shard", pairs)
            images += [a, b, swap(a), swap(b)]
            slots += [(k, 0), (k, 1), (-k, 1), (-k, 0)]
            if k == 1 or k == groups - 1:
                stage_images.append(images)
                stage_slots.append(tuple(slots))
                images, slots = [], []

        packed = call(packed_kernel, struct(((groups - 1) * part, lanes + features)), (), messages)
        shared = [packed] + [share(packed, j) for j in range(1, sharers)]
        mine, out_mine = call(
            functools.partial(gathered_kernel, (groups, rows, sharers, devices, 3 * width)),
            [struct((groups * rows, lanes)), struct((groups * rows, features))],
            (),
            (own_block, w_out, *shared),
            [pltpu.VMEM(((groups - 1) * rows, lanes + features), F32)],
        )
        other, out_other = swap(mine), swap(out_mine)
        join = functools.partial(joined_kernel, (groups, members, rows))
        weights = call(join, struct((features, lanes)), (), (mine, other))
        table = sum(
            x[k * rows : k * rows + devices, 3 * width : 3 * width + devices].astype(F32)
            for x in (mine, other)
            for k in range(groups)
        )
        out_weights = lambda: call(join, struct((features, features)), (), (out_mine, out_other))
    else:
        gather = lambda x: lax.all_gather(x, "shard", axis=0, tiled=True)
        own = lax.axis_index("shard") // members
        columns = lambda w: lax.dynamic_slice_in_dim(gather(w), own * width, width, 1)
        weights = jnp.concatenate([columns(w) for w in (w_key, w_value, w_query)], axis=1)
        table = call(table_kernel, struct((round_up(devices, 16), 128)), small, ())
        table = jnp.sum(gather(table[None])[:, :devices, :devices].astype(F32), axis=0)
        normed = call(norm_kernel, struct((length, features)), (), (tokens[0], norm_gain))
        normed = gather(normed[None])
        stage_images.append([normed[i] for i in range(devices)])
        stage_slots.append(tuple((None, i) for i in range(devices)))
        out_weights = lambda: gather(w_out)

    state_shapes = (
        struct((devices, length, width)),
        struct((devices, width + ONES, length)),
        struct((groups, width, heads * length)),
        struct((groups, max(heads // 2, 1), 2 * HEAD_DIM, 2 * length), F32),
        struct((groups, HEAD_DIM, length), F32),
    )
    part_shape = struct((length // 2, 2 * width))
    every = tuple(range(groups))
    far, near = every[: groups // 2 - 1 : -1], every[: groups // 2]
    if relayed:
        stages = (
            ((-1, 1), True, (0, groups), (), True),
            ((1, groups), True, (0, groups), far + near, False),
        )
    else:
        stages = (((-1, groups), True, (0, groups), every, False),)
    parts, state = {}, ()
    for s, (reach, fresh, asked, sent, keep) in enumerate(stages):
        cfg = (groups, members, heads, reach, fresh, stage_slots[s], asked, sent, keep)
        scratch = [pltpu.VMEM((groups, members * length, features), BF16), pltpu.SMEM((groups * devices + 1,), jnp.int32)]
        shapes = [part_shape] * len(sent)
        if keep:
            shapes += state_shapes
        else:
            scratch = [pltpu.VMEM(x.shape, x.dtype) for x in state_shapes[0 if fresh else 3 :]] + scratch
        results = call(
            functools.partial(attention_kernel, cfg),
            shapes,
            (table,),
            (weights, *stage_images[s], *state),
            scratch,
            megabytes=24 if relayed else 60,
        )
        for k, part in zip(sent, results):
            parts[k] = exchange(part, k) if k else part
        state = results[len(sent) :]
    parts = [parts[k] for k in every]
    out = call(
        functools.partial(output_kernel, (groups, members)),
        struct((length, features)),
        (),
        (out_weights(), *parts),
        [pltpu.VMEM((groups, length, width), BF16)],
    )
    return out[None]


def solution(mesh):
    in_specs = (
        P(("group", "shard"), None, None),
        P(),
        P("shard", None),
        P("shard", None),
        P("shard", None),
        P("shard", None),
        P("group", None),
        P(("group", "shard"), None),
        P(("group", "shard")),
        P(("group", "shard"), None),
    )
    out_specs = P(("group", "shard"), None, None)
    return jax.shard_map(
        functools.partial(shards, dict(mesh.shape)),
        mesh=mesh,
        in_specs=in_specs,
        out_specs=out_specs,
        check_vma=False,
    )
```
